512 devices in a mesh: wide: 64 (over z, x), narrow: 8 (over y, core).
Axes of the slice: x: 4, y: 4, z: 16, core: 2. Of those that a mesh axis runs over, the one named last changes fastest.
Arguments:
- sublevel_symbol_entries: bfloat16 [1024, 4, 4096], P('wide', None, 'narrow'), may hold values from -160 to 160
- prior_symbol_memory: bfloat16 [1024, 4096], P('wide', 'narrow'), may hold values from -6 to 6
- entry_scaling_multiplier: float32 [4096], P('narrow'), may hold values from 0.25 to 1.75
- entry_scaling_offset: float32 [4096], P('narrow'), may hold values from -4 to 4
- learned_blending: float32 [6, 4096], P(None, 'narrow'), may hold values from 0 to 1
- blending_lowering_coefficients: bfloat16 [4096, 160], P('narrow'), may hold values from -0.09375 to 0.09375
- blending_raising_coefficients: bfloat16 [5, 32, 4096], P(None, None, 'narrow'), may hold values from -1 to 1
- fading_lowering_coefficients: bfloat16 [4096, 64], P('narrow'), may hold values from -0.09375 to 0.09375
- fading_raising_coefficients: bfloat16 [64, 4096], P(None, 'wide'), may hold values from -0.75 to 0.75
- learned_fading: float32 [4096], P('wide'), may hold values from -6 to 1
- immediate_item_premium: float32 [4096], P('wide'), may hold values from -3 to 3
- acceptor_projection: bfloat16 [4096, 4096], P('narrow', 'wide'), may hold values from -0.09375 to 0.09375
- lookup_projection: bfloat16 [4096, 4096], P('narrow', 'wide'), may hold values from -0.09375 to 0.09375
- payload_projection: bfloat16 [4096, 4096], P('narrow', 'wide'), may hold values from -0.09375 to 0.09375
- gating_projection: bfloat16 [4096, 4096], P('narrow', 'wide'), may hold values from -0.09375 to 0.09375
- emission_projection: bfloat16 [4096, 4096], P(None, 'wide'), may hold values from -0.09375 to 0.09375
- group_scaling_multiplier: float32 [4096], P('wide'), may hold values from 0.25 to 1.75
- group_scaling_offset: float32 [4096], P('wide'), may hold values from -4 to 4
- dialogue_group_memory: float32 [262144, 1024], P('wide', 'narrow'), may hold values from -6 to 6
Outputs:
- mixing_output: bfloat16 [1024, 4, 4096], P('narrow', None, 'wide')
- final_state: float32 [262144, 1024], P('wide', 'narrow')
The draws below stay inside these ranges and needn't reach their ends.
All inputs are finite; a program needn't handle non-finite values.
Results may differ from the reference program's by a relative error of at most 0.034.
Values may be sent and summed in bfloat16 or wider, within the bound.
A program may use at most 64 MiB of HBM per device.

```python
import math
import jax
import jax.numpy as jnp
from jax import lax

NUM_CHANNEL_SETS = 64
CHANNEL_SPAN = 64
MIXING_RANK = 32
DECAY_RANK = 64
PARALLEL_CHATS = 1024
DECODE_MOVES = 4
FEATURE_EXTENT = 4096
N_NARROW = 8


def feature_draw(key, shape):
    first, second, third = jax.random.split(key, 3)
    columns = shape[-1]
    ramp = 3.0 ** (jnp.arange(columns, dtype=jnp.float32) / columns)
    column_scale = ramp * jnp.exp(jax.random.uniform(first, (columns,), jnp.float32, 0.0, math.log(3.3)))
    row_scale = jnp.exp(jax.random.uniform(second, (shape[0],) + (1,) * (len(shape) - 1), jnp.float32, 0.0, math.log(10.0)))
    base = jnp.clip(jax.random.normal(third, shape, jnp.float32), -5.0, 5.0)
    return (base * column_scale * row_scale * 0.3).astype(jnp.bfloat16)


def draw_sublevel_symbol_entries(key, part):
    return feature_draw(jax.random.fold_in(key, 11), (PARALLEL_CHATS, DECODE_MOVES, FEATURE_EXTENT))


def block_levels(own_key, shape, pieces, low, top_value):
    level, own = 1.0, jax.random.fold_in(own_key, 6)
    for position, parts in pieces:
        steps = jnp.exp(jax.random.uniform(jax.random.fold_in(own, position), (parts,), jnp.float32, low / len(pieces), top_value / len(pieces)))
        level = level * jnp.repeat(steps, shape[position] // parts).reshape([-1 if axis == position else 1 for axis in range(len(shape))])
    return level


def bell_draw(key, dims, scale, most, cuts=(), held_as=jnp.bfloat16):
    gain = block_levels(key, dims, cuts, -0.22, 0.18) if cuts else 1.0
    values = jax.random.normal(key, dims, jnp.float32) * scale * gain
    return jnp.minimum(jnp.maximum(values, -most), most).astype(held_as)


def setup_inputs(seed: int = 0) -> dict:
    key_of = jax.random.split(jax.random.key(seed), 20)
    sublevel_symbol_entries = draw_sublevel_symbol_entries(jax.random.fold_in(key_of[19], 71), 0)
    prior_symbol_memory = bell_draw(key_of[1], (PARALLEL_CHATS, FEATURE_EXTENT), 1.0, 6.0, ((0, 64), (1, 8)))
    entry_scaling_multiplier = jnp.clip(1.0 + 0.15 * jax.random.normal(key_of[2], (FEATURE_EXTENT,), jnp.float32), 0.25, 1.75)
    entry_scaling_offset = bell_draw(key_of[3], (FEATURE_EXTENT,), 0.3, 4.0, ((0, 8),), jnp.float32)
    learned_blending = jnp.clip(1.0 * jax.random.uniform(key_of[4], (6, FEATURE_EXTENT), jnp.float32) ** block_levels(key_of[4], (6, FEATURE_EXTENT), ((1, 8),), -0.2, 0.2), 0.0, 1.0)
    blending_lowering_coefficients = bell_draw(key_of[5], (FEATURE_EXTENT, 5 * MIXING_RANK), FEATURE_EXTENT ** -0.5, 0.09375, ((0, 8),))
    blending_raising_coefficients = bell_draw(key_of[6], (5, MIXING_RANK, FEATURE_EXTENT), MIXING_RANK ** -0.5, 1.0, ((2, 8),))
    fading_lowering_coefficients = bell_draw(key_of[7], (FEATURE_EXTENT, DECAY_RANK), FEATURE_EXTENT ** -0.5, 0.09375, ((0, 8),))
    fading_raising_coefficients = bell_draw(key_of[8], (DECAY_RANK, FEATURE_EXTENT), DECAY_RANK ** -0.5, 0.75, ((1, 64),))
    learned_fading = jnp.clip(-6.0 + 7.0 * jax.random.uniform(key_of[9], (FEATURE_EXTENT,), jnp.float32) ** block_levels(key_of[9], (FEATURE_EXTENT,), ((0, 64),), -0.2, 0.2), -6.0, 1.0)
    immediate_item_premium = bell_draw(key_of[10], (FEATURE_EXTENT,), 0.5, 3.0, ((0, 64),), jnp.float32)
    acceptor_projection = bell_draw(key_of[11], (FEATURE_EXTENT, FEATURE_EXTENT), FEATURE_EXTENT ** -0.5, 0.09375, ((0, 8), (1, 64)))
    lookup_projection = bell_draw(key_of[12], (FEATURE_EXTENT, FEATURE_EXTENT), FEATURE_EXTENT ** -0.5, 0.09375, ((0, 8), (1, 64)))
    payload_projection = bell_draw(key_of[13], (FEATURE_EXTENT, FEATURE_EXTENT), FEATURE_EXTENT ** -0.5, 0.09375, ((0, 8), (1, 64)))
    gating_projection = bell_draw(key_of[14], (FEATURE_EXTENT, FEATURE_EXTENT), FEATURE_EXTENT ** -0.5, 0.09375, ((0, 8), (1, 64)))
    emission_projection = bell_draw(key_of[15], (FEATURE_EXTENT, FEATURE_EXTENT), FEATURE_EXTENT ** -0.5, 0.09375, ((1, 64),))
    group_scaling_multiplier = jnp.clip(1.0 + 0.15 * jax.random.normal(key_of[16], (FEATURE_EXTENT,), jnp.float32), 0.25, 1.75)
    group_scaling_offset = bell_draw(key_of[17], (FEATURE_EXTENT,), 0.3, 4.0, ((0, 64),), jnp.float32)
    dialogue_group_memory = bell_draw(key_of[18], (FEATURE_EXTENT * CHANNEL_SPAN, PARALLEL_CHATS), 1.0, 6.0, ((0, 64), (1, 8)), jnp.float32)
    return dict(sublevel_symbol_entries=sublevel_symbol_entries, prior_symbol_memory=prior_symbol_memory, entry_scaling_multiplier=entry_scaling_multiplier, entry_scaling_offset=entry_scaling_offset, learned_blending=learned_blending, blending_lowering_coefficients=blending_lowering_coefficients, blending_raising_coefficients=blending_raising_coefficients, fading_lowering_coefficients=fading_lowering_coefficients, fading_raising_coefficients=fading_raising_coefficients, learned_fading=learned_fading, immediate_item_premium=immediate_item_premium, acceptor_projection=acceptor_projection, lookup_projection=lookup_projection, payload_projection=payload_projection, gating_projection=gating_projection, emission_projection=emission_projection, group_scaling_multiplier=group_scaling_multiplier, group_scaling_offset=group_scaling_offset, dialogue_group_memory=dialogue_group_memory)


def flattened_product(left, right):
    shape = left.shape
    result = jnp.dot(left.reshape(-1, shape[-1]), right, preferred_element_type=jnp.float32)
    return result.reshape(shape[:-1] + (right.shape[-1],))

def blocked_dot(left, right):
    width = left.shape[-1] // N_NARROW
    total = jnp.zeros(left.shape[:-1] + (right.shape[-1],), jnp.float32)
    for block in range(N_NARROW):
        term = flattened_product(left[..., block * width:(block + 1) * width], right[block * width:(block + 1) * width])
        total = total + lax.optimization_barrier(term.astype(jnp.bfloat16)).astype(jnp.float32)
    return total

def solitary_channel_set(entry_lines):
    acceptor_lines, group_lookup, group_payload, retention_multiplier, present_symbol, group_reward = entry_lines
    outputs = []
    for index in range(DECODE_MOVES):
        present_acceptor = acceptor_lines[:, index].T
        key_now = group_lookup[:, index].T
        value_now = group_payload[:, index].T
        forget_now = retention_multiplier[:, index].T
        dyadic_tensor = key_now[:, None, :] * value_now[None, :, :]
        memory_retrieval = lax.optimization_barrier(jnp.sum(present_acceptor[:, None, :] * (present_symbol + group_reward[:, None, None] * dyadic_tensor), 0))
        present_symbol = forget_now[:, None, :] * present_symbol + dyadic_tensor
        center = lax.optimization_barrier(jnp.mean(memory_retrieval, 0, keepdims=True))
        offset = memory_retrieval - center
        outputs.append(offset * lax.rsqrt(lax.optimization_barrier(jnp.mean(offset * offset, 0, keepdims=True)) + 0.00064))
    return (jnp.stack(outputs, 0), present_symbol)

def reference(sublevel_symbol_entries, prior_symbol_memory, entry_scaling_multiplier, entry_scaling_offset, learned_blending, blending_lowering_coefficients, blending_raising_coefficients, fading_lowering_coefficients, fading_raising_coefficients, learned_fading, immediate_item_premium, acceptor_projection, lookup_projection, payload_projection, gating_projection, emission_projection, group_scaling_multiplier, group_scaling_offset, dialogue_group_memory):
    floats = sublevel_symbol_entries.astype(jnp.float32)
    center = lax.optimization_barrier(jnp.sum(floats, -1, keepdims=True)) / FEATURE_EXTENT
    spread = lax.optimization_barrier(jnp.sum(floats * floats, -1, keepdims=True)) / FEATURE_EXTENT - center * center
    normed = ((floats - center) * lax.rsqrt(spread + 1e-05) * entry_scaling_multiplier + entry_scaling_offset).astype(jnp.bfloat16)
    previous = jnp.concatenate([prior_symbol_memory[:, None], normed[:, :-1]], 1)
    normalized_float = normed.astype(jnp.float32)
    shifted_input = previous.astype(jnp.float32) - normalized_float
    blended = (normalized_float + shifted_input * learned_blending[0]).astype(jnp.bfloat16)
    hidden_activation = jnp.tanh(flattened_product(blended, blending_lowering_coefficients)).astype(jnp.bfloat16)
    mixing_values = []
    for selector_index in range(5):
        low_rank_update = flattened_product(hidden_activation[..., selector_index * MIXING_RANK:(selector_index + 1) * MIXING_RANK], blending_raising_coefficients[selector_index])
        mixing_values.append((normalized_float + shifted_input * (learned_blending[selector_index + 1] + low_rank_update)).astype(jnp.bfloat16))
    decay_hidden = jnp.tanh(flattened_product(mixing_values[0], fading_lowering_coefficients)).astype(jnp.bfloat16)
    shrink_coefficient = jnp.exp(-jnp.exp(learned_fading + flattened_product(decay_hidden, fading_raising_coefficients)))
    weights = (acceptor_projection, lookup_projection, payload_projection, gating_projection)
    transformed_outcome = [blocked_dot(mixing_values[selector_index + 1], weights[selector_index]) for selector_index in range(4)]

    def channel_set_first(array):
        return array.reshape(PARALLEL_CHATS, DECODE_MOVES, NUM_CHANNEL_SETS, CHANNEL_SPAN).transpose(2, 0, 1, 3)
    channel_set_recalls = dialogue_group_memory.reshape(NUM_CHANNEL_SETS, CHANNEL_SPAN, CHANNEL_SPAN, PARALLEL_CHATS)
    recalled_vectors, concluding_outcome = lax.map(solitary_channel_set, (channel_set_first(transformed_outcome[0]), channel_set_first(transformed_outcome[1]), channel_set_first(transformed_outcome[2]), channel_set_first(shrink_coefficient), channel_set_recalls, immediate_item_premium.reshape(NUM_CHANNEL_SETS, CHANNEL_SPAN)))
    squashed_vector = recalled_vectors.transpose(3, 1, 0, 2).reshape(PARALLEL_CHATS, DECODE_MOVES, FEATURE_EXTENT)
    gated = ((squashed_vector * group_scaling_multiplier + group_scaling_offset) * jax.nn.silu(transformed_outcome[3])).astype(jnp.bfloat16)
    mixing_output = flattened_product(gated, emission_projection).astype(jnp.bfloat16)
    return (mixing_output, concluding_outcome.reshape(FEATURE_EXTENT * CHANNEL_SPAN, PARALLEL_CHATS))
```

```python
import jax
import jax.numpy as jnp
from jax import lax
from jax.sharding import PartitionSpec as P

CHANNEL_SPAN = 64
FEATURE_EXTENT = 4096


def per_device(
    sublevel_symbol_entries,
    prior_symbol_memory,
    entry_scaling_multiplier,
    entry_scaling_offset,
    learned_blending,
    blending_lowering_coefficients,
    blending_raising_coefficients,
    fading_lowering_coefficients,
    fading_raising_coefficients,
    learned_fading,
    immediate_item_premium,
    acceptor_projection,
    lookup_projection,
    payload_projection,
    gating_projection,
    emission_projection,
    group_scaling_multiplier,
    group_scaling_offset,
    dialogue_group_memory,
):
    rank = blending_raising_coefficients.shape[1]
    narrow_rows = dialogue_group_memory.shape[1]
    local_width = emission_projection.shape[1]
    group_partition = local_width // CHANNEL_SPAN
    sessions, steps, features = sublevel_symbol_entries.shape
    weights = (acceptor_projection, lookup_projection, payload_projection, gating_projection)

    floats = sublevel_symbol_entries.astype(jnp.float32)
    stats = lax.psum(
        jnp.stack([jnp.sum(floats, -1), jnp.sum(floats * floats, -1)], 0), "narrow"
    )
    center = stats[0][..., None] / FEATURE_EXTENT
    spread = stats[1][..., None] / FEATURE_EXTENT - center * center
    normed = (
        (floats - center) * lax.rsqrt(spread + 1e-05) * entry_scaling_multiplier
        + entry_scaling_offset
    ).astype(jnp.bfloat16)
    previous = jnp.concatenate([prior_symbol_memory[:, None], normed[:, :-1]], 1)
    normalized_float = normed.astype(jnp.float32)
    shifted_input = previous.astype(jnp.float32) - normalized_float
    blended = (normalized_float + shifted_input * learned_blending[0]).astype(jnp.bfloat16)
    partial_mix = jnp.einsum(
        "smd,dr->smr", blended, blending_lowering_coefficients,
        preferred_element_type=jnp.float32,
    )
    hidden_activation = jnp.tanh(lax.psum(partial_mix, "narrow")).astype(jnp.bfloat16)
    decay_shift = jnp.einsum(
        "smr,rd->smd", hidden_activation[..., :rank], blending_raising_coefficients[0],
        preferred_element_type=jnp.float32,
    )
    decay_mix = (
        normalized_float + shifted_input * (learned_blending[1] + decay_shift)
    ).astype(jnp.bfloat16)
    partial_decay = jnp.einsum(
        "smd,dr->smr", decay_mix, fading_lowering_coefficients,
        preferred_element_type=jnp.float32,
    )
    decay_hidden = jnp.tanh(lax.psum(partial_decay, "narrow")).astype(jnp.bfloat16)
    small = jnp.concatenate([hidden_activation[..., rank:], decay_hidden], -1)
    small_width = small.shape[-1]

    packed = jnp.concatenate(
        [
            normed.reshape(sessions, steps * features),
            prior_symbol_memory,
            small.reshape(sessions, steps * small_width),
        ],
        -1,
    )
    packed_all = lax.all_gather(packed, "wide", axis=0, tiled=True)
    all_sessions = packed_all.shape[0]
    normed_all = packed_all[:, : steps * features].reshape(all_sessions, steps, features)
    prior_all = packed_all[:, steps * features : (steps + 1) * features]
    small_all = packed_all[:, (steps + 1) * features :].reshape(
        all_sessions, steps, small_width
    )
    previous_all = jnp.concatenate([prior_all[:, None], normed_all[:, :-1]], 1)
    normalized_all = normed_all.astype(jnp.float32)
    shifted_all = previous_all.astype(jnp.float32) - normalized_all
    term_results = []
    for selector_index in range(4):
        low_rank_update = jnp.einsum(
            "smr,rd->smd",
            small_all[..., selector_index * rank : (selector_index + 1) * rank],
            blending_raising_coefficients[selector_index + 1],
            preferred_element_type=jnp.float32,
        )
        mixed_input = (
            normalized_all
            + shifted_all * (learned_blending[selector_index + 2] + low_rank_update)
        ).astype(jnp.bfloat16)
        term_results.append(
            jnp.einsum(
                "smd,de->sme", mixed_input, weights[selector_index],
                preferred_element_type=jnp.float32,
            ).astype(jnp.bfloat16)
        )
    projected = lax.psum_scatter(
        jnp.concatenate(term_results, -1), "narrow", scatter_dimension=0, tiled=True
    ).astype(jnp.float32)

    rows_start = lax.axis_index("narrow") * narrow_rows
    decay_rows = lax.dynamic_slice_in_dim(small_all[..., 4 * rank :], rows_start, narrow_rows, 0)
    decay_log = learned_fading + jnp.einsum(
        "smr,rd->smd", decay_rows, fading_raising_coefficients,
        preferred_element_type=jnp.float32,
    )
    shrink_coefficient = jnp.exp(-jnp.exp(decay_log))

    def channel_set_first(block):
        return block.reshape(narrow_rows, group_partition, CHANNEL_SPAN).transpose(1, 2, 0)

    state = dialogue_group_memory.reshape(group_partition, CHANNEL_SPAN, CHANNEL_SPAN, narrow_rows)
    reward = immediate_item_premium.reshape(group_partition, CHANNEL_SPAN)
    pieces = []
    for index in range(steps):
        acceptor = channel_set_first(projected[:, index, :local_width])
        key_now = channel_set_first(projected[:, index, local_width : 2 * local_width])
        value_now = channel_set_first(projected[:, index, 2 * local_width : 3 * local_width])
        gate_now = projected[:, index, 3 * local_width :]
        forget_now = channel_set_first(shrink_coefficient[:, index])
        dyadic = key_now[:, :, None, :] * value_now[:, None, :, :]
        retrieval = jnp.sum(
            acceptor[:, :, None, :] * (state + reward[:, :, None, None] * dyadic), 1
        )
        state = forget_now[:, :, None, :] * state + dyadic
        center_r = jnp.mean(retrieval, 1, keepdims=True)
        offset = retrieval - center_r
        scaled = offset * lax.rsqrt(jnp.mean(offset * offset, 1, keepdims=True) + 0.00064)
        squashed = scaled.transpose(2, 0, 1).reshape(narrow_rows, local_width)
        pieces.append(
            (
                (squashed * group_scaling_multiplier + group_scaling_offset)
                * jax.nn.silu(gate_now)
            ).astype(jnp.bfloat16)
        )
    gated = jnp.stack(pieces, 1)
    mixing_output = jnp.einsum(
        "smc,ce->sme",
        lax.all_gather(gated, "wide", axis=2, tiled=True),
        emission_projection,
        preferred_element_type=jnp.float32,
    ).astype(jnp.bfloat16)
    return (
        mixing_output,
        state.reshape(group_partition * CHANNEL_SPAN * CHANNEL_SPAN, narrow_rows),
    )


def solution(mesh):
    placed = (
        P("wide", None, "narrow"),
        P("wide", "narrow"),
        P("narrow"),
        P("narrow"),
        P(None, "narrow"),
        P("narrow", None),
        P(None, None, "narrow"),
        P("narrow", None),
        P(None, "wide"),
        P("wide"),
        P("wide"),
        P("narrow", "wide"),
        P("narrow", "wide"),
        P("narrow", "wide"),
        P("narrow", "wide"),
        P(None, "wide"),
        P("wide"),
        P("wide"),
        P("wide", "narrow"),
    )
    return jax.shard_map(
        per_device,
        mesh=mesh,
        in_specs=placed,
        out_specs=(P("narrow", None, "wide"), P("wide", "narrow")),
        check_vma=False,
    )
```

```python
import jax
import jax.numpy as jnp
from jax import lax
from jax.sharding import PartitionSpec as P

CHANNEL_SPAN = 64
FEATURE_EXTENT = 4096


def per_device(
    sublevel_symbol_entries,
    prior_symbol_memory,
    entry_scaling_multiplier,
    entry_scaling_offset,
    learned_blending,
    blending_lowering_coefficients,
    blending_raising_coefficients,
    fading_lowering_coefficients,
    fading_raising_coefficients,
    learned_fading,
    immediate_item_premium,
    acceptor_projection,
    lookup_projection,
    payload_projection,
    gating_projection,
    emission_projection,
    group_scaling_multiplier,
    group_scaling_offset,
    dialogue_group_memory,
):
    rank = blending_raising_coefficients.shape[1]
    narrow_rows = dialogue_group_memory.shape[1]
    local_width = emission_projection.shape[1]
    group_partition = local_width // CHANNEL_SPAN
    sessions, steps, features = sublevel_symbol_entries.shape
    weights = (acceptor_projection, lookup_projection, payload_projection, gating_projection)

    floats = sublevel_symbol_entries.astype(jnp.float32)
    stats = lax.psum(
        jnp.stack([jnp.sum(floats, -1), jnp.sum(floats * floats, -1)], 0), "narrow"
    )
    center = stats[0][..., None] / FEATURE_EXTENT
    spread = stats[1][..., None] / FEATURE_EXTENT - center * center
    normed = (
        (floats - center) * lax.rsqrt(spread + 1e-05) * entry_scaling_multiplier
        + entry_scaling_offset
    ).astype(jnp.bfloat16)
    previous = jnp.concatenate([prior_symbol_memory[:, None], normed[:, :-1]], 1)
    normalized_float = normed.astype(jnp.float32)
    shifted_input = previous.astype(jnp.float32) - normalized_float
    blended = (normalized_float + shifted_input * learned_blending[0]).astype(jnp.bfloat16)
    partial_mix = jnp.einsum(
        "smd,dr->smr", blended, blending_lowering_coefficients,
        preferred_element_type=jnp.float32,
    )
    hidden_activation = jnp.tanh(lax.psum(partial_mix, "narrow")).astype(jnp.bfloat16)
    decay_shift = jnp.einsum(
        "smr,rd->smd", hidden_activation[..., :rank], blending_raising_coefficients[0],
        preferred_element_type=jnp.float32,
    )
    decay_mix = (
        normalized_float + shifted_input * (learned_blending[1] + decay_shift)
    ).astype(jnp.bfloat16)
    partial_decay = jnp.einsum(
        "smd,dr->smr", decay_mix, fading_lowering_coefficients,
        preferred_element_type=jnp.float32,
    )
    decay_hidden = jnp.tanh(lax.psum(partial_decay, "narrow")).astype(jnp.bfloat16)
    small = jnp.concatenate([hidden_activation[..., rank:], decay_hidden], -1)
    small_width = small.shape[-1]

    packed = jnp.concatenate(
        [
            normed.reshape(sessions, steps * features),
            prior_symbol_memory,
            small.reshape(sessions, steps * small_width),
        ],
        -1,
    )
    packed_all = lax.all_gather(
        lax.all_gather(packed, "x", axis=0, tiled=True), "z", axis=0, tiled=True
    )
    all_sessions = packed_all.shape[0]
    normed_all = packed_all[:, : steps * features].reshape(all_sessions, steps, features)
    prior_all = packed_all[:, steps * features : (steps + 1) * features]
    small_all = packed_all[:, (steps + 1) * features :].reshape(
        all_sessions, steps, small_width
    )
    previous_all = jnp.concatenate([prior_all[:, None], normed_all[:, :-1]], 1)
    normalized_all = normed_all.astype(jnp.float32)
    shifted_all = previous_all.astype(jnp.float32) - normalized_all
    term_results = []
    for selector_index in range(4):
        low_rank_update = jnp.einsum(
            "smr,rd->smd",
            small_all[..., selector_index * rank : (selector_index + 1) * rank],
            blending_raising_coefficients[selector_index + 1],
            preferred_element_type=jnp.float32,
        )
        mixed_input = (
            normalized_all
            + shifted_all * (learned_blending[selector_index + 2] + low_rank_update)
        ).astype(jnp.bfloat16)
        term_results.append(
            jnp.einsum(
                "smd,de->sme", mixed_input, weights[selector_index],
                preferred_element_type=jnp.float32,
            ).astype(jnp.bfloat16)
        )
    projected = lax.psum_scatter(
        jnp.concatenate(term_results, -1), "narrow", scatter_dimension=0, tiled=True
    ).astype(jnp.float32)

    rows_start = lax.axis_index("narrow") * narrow_rows
    decay_rows = lax.dynamic_slice_in_dim(small_all[..., 4 * rank :], rows_start, narrow_rows, 0)
    decay_log = learned_fading + jnp.einsum(
        "smr,rd->smd", decay_rows, fading_raising_coefficients,
        preferred_element_type=jnp.float32,
    )
    shrink_coefficient = jnp.exp(-jnp.exp(decay_log))

    def channel_set_first(block):
        return block.reshape(narrow_rows, group_partition, CHANNEL_SPAN).transpose(1, 2, 0)

    state = dialogue_group_memory.reshape(group_partition, CHANNEL_SPAN, CHANNEL_SPAN, narrow_rows)
    reward = immediate_item_premium.reshape(group_partition, CHANNEL_SPAN)
    pieces = []
    for index in range(steps):
        acceptor = channel_set_first(projected[:, index, :local_width])
        key_now = channel_set_first(projected[:, index, local_width : 2 * local_width])
        value_now = channel_set_first(projected[:, index, 2 * local_width : 3 * local_width])
        gate_now = projected[:, index, 3 * local_width :]
        forget_now = channel_set_first(shrink_coefficient[:, index])
        dyadic = key_now[:, :, None, :] * value_now[:, None, :, :]
        retrieval = jnp.sum(
            acceptor[:, :, None, :] * (state + reward[:, :, None, None] * dyadic), 1
        )
        state = forget_now[:, :, None, :] * state + dyadic
        center_r = jnp.mean(retrieval, 1, keepdims=True)
        offset = retrieval - center_r
        scaled = offset * lax.rsqrt(jnp.mean(offset * offset, 1, keepdims=True) + 0.00064)
        squashed = scaled.transpose(2, 0, 1).reshape(narrow_rows, local_width)
        pieces.append(
            (
                (squashed * group_scaling_multiplier + group_scaling_offset)
                * jax.nn.silu(gate_now)
            ).astype(jnp.bfloat16)
        )
    gated = jnp.stack(pieces, 1)
    mixing_output = jnp.einsum(
        "smc,ce->sme",
        lax.all_gather(
            lax.all_gather(gated, "x", axis=2, tiled=True), "z", axis=2, tiled=True
        ),
        emission_projection,
        preferred_element_type=jnp.float32,
    ).astype(jnp.bfloat16)
    return (
        mixing_output,
        state.reshape(group_partition * CHANNEL_SPAN * CHANNEL_SPAN, narrow_rows),
    )


def solution(mesh):
    wide_size = mesh.shape["wide"]
    x_size = 4 if wide_size % 4 == 0 else 1
    split = jax.sharding.Mesh(
        mesh.devices.reshape(wide_size // x_size, x_size, mesh.shape["narrow"]),
        ("z", "x", "narrow"),
    )
    wide = ("z", "x")
    placed = (
        P(wide, None, "narrow"),
        P(wide, "narrow"),
        P("narrow"),
        P("narrow"),
        P(None, "narrow"),
        P("narrow", None),
        P(None, None, "narrow"),
        P("narrow", None),
        P(None, wide),
        P(wide),
        P(wide),
        P("narrow", wide),
        P("narrow", wide),
        P("narrow", wide),
        P("narrow", wide),
        P(None, wide),
        P(wide),
        P(wide),
        P(wide, "narrow"),
    )
    return jax.shard_map(
        per_device,
        mesh=split,
        in_specs=placed,
        out_specs=(P("narrow", None, wide), P(wide, "narrow")),
        check_vma=False,
    )
```

```python
import jax
import jax.numpy as jnp
from jax import lax
from jax.sharding import PartitionSpec as P

CHANNEL_SPAN = 64
FEATURE_EXTENT = 4096


def per_device(
    sublevel_symbol_entries,
    prior_symbol_memory,
    entry_scaling_multiplier,
    entry_scaling_offset,
    learned_blending,
    blending_lowering_coefficients,
    blending_raising_coefficients,
    fading_lowering_coefficients,
    fading_raising_coefficients,
    learned_fading,
    immediate_item_premium,
    acceptor_projection,
    lookup_projection,
    payload_projection,
    gating_projection,
    emission_projection,
    group_scaling_multiplier,
    group_scaling_offset,
    dialogue_group_memory,
):
    rank = blending_raising_coefficients.shape[1]
    narrow_rows = dialogue_group_memory.shape[1]
    local_width = emission_projection.shape[1]
    group_partition = local_width // CHANNEL_SPAN
    sessions, steps, features = sublevel_symbol_entries.shape
    weights = (acceptor_projection, lookup_projection, payload_projection, gating_projection)

    floats = sublevel_symbol_entries.astype(jnp.float32)
    stats = lax.psum(
        jnp.stack([jnp.sum(floats, -1), jnp.sum(floats * floats, -1)], 0), "narrow"
    )
    center = stats[0][..., None] / FEATURE_EXTENT
    spread = stats[1][..., None] / FEATURE_EXTENT - center * center
    normed = (
        (floats - center) * lax.rsqrt(spread + 1e-05) * entry_scaling_multiplier
        + entry_scaling_offset
    ).astype(jnp.bfloat16)
    previous = jnp.concatenate([prior_symbol_memory[:, None], normed[:, :-1]], 1)
    normalized_float = normed.astype(jnp.float32)
    shifted_input = previous.astype(jnp.float32) - normalized_float
    blended = (normalized_float + shifted_input * learned_blending[0]).astype(jnp.bfloat16)
    partial_mix = jnp.einsum(
        "smd,dr->smr", blended, blending_lowering_coefficients,
        preferred_element_type=jnp.float32,
    )
    hidden_activation = jnp.tanh(lax.psum(partial_mix, "narrow")).astype(jnp.bfloat16)
    decay_shift = jnp.einsum(
        "smr,rd->smd", hidden_activation[..., :rank], blending_raising_coefficients[0],
        preferred_element_type=jnp.float32,
    )
    decay_mix = (
        normalized_float + shifted_input * (learned_blending[1] + decay_shift)
    ).astype(jnp.bfloat16)
    partial_decay = jnp.einsum(
        "smd,dr->smr", decay_mix, fading_lowering_coefficients,
        preferred_element_type=jnp.float32,
    )
    decay_hidden = jnp.tanh(lax.psum(partial_decay, "narrow")).astype(jnp.bfloat16)
    small = jnp.concatenate([hidden_activation[..., rank:], decay_hidden], -1)
    small_width = small.shape[-1]

    packed = jnp.concatenate(
        [prior_symbol_memory]
        + [normed[:, index] for index in range(steps)]
        + [small.reshape(sessions, steps * small_width)],
        -1,
    )
    packed_all = lax.all_gather(
        lax.all_gather(packed, "x", axis=0, tiled=True), "z", axis=0, tiled=True
    )
    small_start = (steps + 1) * features
    term_results = []
    for index in range(steps):
        previous_now = packed_all[:, index * features : (index + 1) * features]
        normed_now = packed_all[:, (index + 1) * features : (index + 2) * features]
        normalized_now = normed_now.astype(jnp.float32)
        shifted_now = previous_now.astype(jnp.float32) - normalized_now
        small_now = small_start + index * small_width
        for selector_index in range(4):
            low_rank_update = jnp.dot(
                packed_all[:, small_now + selector_index * rank : small_now + (selector_index + 1) * rank],
                blending_raising_coefficients[selector_index + 1],
                preferred_element_type=jnp.float32,
            )
            mixed_input = (
                normalized_now
                + shifted_now * (learned_blending[selector_index + 2] + low_rank_update)
            ).astype(jnp.bfloat16)
            term_results.append(
                jnp.dot(
                    mixed_input, weights[selector_index], preferred_element_type=jnp.float32
                ).astype(jnp.bfloat16)
            )
    projected = lax.psum_scatter(
        jnp.concatenate(term_results, -1), "narrow", scatter_dimension=0, tiled=True
    ).astype(jnp.float32).reshape(narrow_rows, steps, 4 * local_width)

    rows_start = lax.axis_index("narrow") * narrow_rows
    own_rows = lax.dynamic_slice_in_dim(packed_all[:, small_start:], rows_start, narrow_rows, 0)
    decay_rows = own_rows.reshape(narrow_rows, steps, small_width)[..., 4 * rank :]
    decay_log = learned_fading + jnp.einsum(
        "smr,rd->smd", decay_rows, fading_raising_coefficients,
        preferred_element_type=jnp.float32,
    )
    shrink_coefficient = jnp.exp(-jnp.exp(decay_log))

    def channel_set_first(block):
        return block.reshape(narrow_rows, group_partition, CHANNEL_SPAN).transpose(1, 2, 0)

    state = dialogue_group_memory.reshape(group_partition, CHANNEL_SPAN, CHANNEL_SPAN, narrow_rows)
    reward = immediate_item_premium.reshape(group_partition, CHANNEL_SPAN)
    pieces = []
    for index in range(steps):
        acceptor = channel_set_first(projected[:, index, :local_width])
        key_now = channel_set_first(projected[:, index, local_width : 2 * local_width])
        value_now = channel_set_first(projected[:, index, 2 * local_width : 3 * local_width])
        gate_now = projected[:, index, 3 * local_width :]
        forget_now = channel_set_first(shrink_coefficient[:, index])
        dyadic = key_now[:, :, None, :] * value_now[:, None, :, :]
        retrieval = jnp.sum(
            acceptor[:, :, None, :] * (state + reward[:, :, None, None] * dyadic), 1
        )
        state = forget_now[:, :, None, :] * state + dyadic
        center_r = jnp.mean(retrieval, 1, keepdims=True)
        offset = retrieval - center_r
        scaled = offset * lax.rsqrt(jnp.mean(offset * offset, 1, keepdims=True) + 0.00064)
        squashed = scaled.transpose(2, 0, 1).reshape(narrow_rows, local_width)
        pieces.append(
            (
                (squashed * group_scaling_multiplier + group_scaling_offset)
                * jax.nn.silu(gate_now)
            ).astype(jnp.bfloat16)
        )
    gated = jnp.stack(pieces, 1).reshape(narrow_rows * steps, local_width).T
    gated_all = lax.all_gather(
        lax.all_gather(gated, "x", axis=0, tiled=True), "z", axis=0, tiled=True
    )
    mixing_output = (
        jnp.einsum(
            "cs,ce->se", gated_all, emission_projection, preferred_element_type=jnp.float32
        )
        .astype(jnp.bfloat16)
        .reshape(narrow_rows, steps, local_width)
    )
    return (
        mixing_output,
        state.reshape(group_partition * CHANNEL_SPAN * CHANNEL_SPAN, narrow_rows),
    )


def solution(mesh):
    wide_size = mesh.shape["wide"]
    x_size = 4 if wide_size % 4 == 0 else 1
    split = jax.sharding.Mesh(
        mesh.devices.reshape(wide_size // x_size, x_size, mesh.shape["narrow"]),
        ("z", "x", "narrow"),
    )
    wide = ("z", "x")
    placed = (
        P(wide, None, "narrow"),
        P(wide, "narrow"),
        P("narrow"),
        P("narrow"),
        P(None, "narrow"),
        P("narrow", None),
        P(None, None, "narrow"),
        P("narrow", None),
        P(None, wide),
        P(wide),
        P(wide),
        P("narrow", wide),
        P("narrow", wide),
        P("narrow", wide),
        P("narrow", wide),
        P(None, wide),
        P(wide),
        P(wide),
        P(wide, "narrow"),
    )
    return jax.shard_map(
        per_device,
        mesh=split,
        in_specs=placed,
        out_specs=(P("narrow", None, wide), P(wide, "narrow")),
        check_vma=False,
    )
```

```python
import jax
import jax.numpy as jnp
from jax import lax
from jax.sharding import PartitionSpec as P
from jax.experimental import pallas as pl
from jax.experimental.pallas import tpu as pltpu

CHANNEL_SPAN = 64
FEATURE_EXTENT = 4096


def narrow_sum_kernel(count, x_ref, o_ref, recv, send_sems, recv_sems):
    me = lax.axis_index("narrow")
    here = (lax.axis_index("z"), lax.axis_index("x"))

    def peer_id(peer):
        return here + (peer,)

    barrier = pltpu.get_barrier_semaphore()
    for peer in range(count):
        @pl.when(peer != me)
        def _():
            pl.semaphore_signal(
                barrier, 1, device_id=peer_id(peer), device_id_type=pl.DeviceIdType.MESH
            )
    pl.semaphore_wait(barrier, count - 1)

    def outgoing(peer):
        return pltpu.make_async_remote_copy(
            src_ref=x_ref,
            dst_ref=recv.at[me],
            send_sem=send_sems.at[peer],
            recv_sem=recv_sems.at[me],
            device_id=peer_id(peer),
            device_id_type=pl.DeviceIdType.MESH,
        )

    def incoming(peer):
        return pltpu.make_async_remote_copy(
            src_ref=x_ref,
            dst_ref=recv.at[peer],
            send_sem=send_sems.at[peer],
            recv_sem=recv_sems.at[peer],
            device_id=peer_id(peer),
            device_id_type=pl.DeviceIdType.MESH,
        )

    for peer in range(count):
        @pl.when(peer != me)
        def _():
            outgoing(peer).start()

    recv[me] = x_ref[...]
    for peer in range(count):
        @pl.when(peer != me)
        def _():
            outgoing(peer).wait_send()
            incoming(peer).wait_recv()

    total = recv[0]
    for peer in range(1, count):
        total = total + recv[peer]
    o_ref[...] = total


def narrow_sum(value, count, collective_id):
    shape = value.shape
    flat = value.reshape(-1, 128)
    summed = pl.pallas_call(
        lambda *refs: narrow_sum_kernel(count, *refs),
        out_shape=jax.ShapeDtypeStruct(flat.shape, flat.dtype),
        in_specs=[pl.BlockSpec(memory_space=pltpu.VMEM)],
        out_specs=pl.BlockSpec(memory_space=pltpu.VMEM),
        scratch_shapes=[
            pltpu.VMEM((count,) + flat.shape, flat.dtype),
            pltpu.SemaphoreType.DMA((count,)),
            pltpu.SemaphoreType.DMA((count,)),
        ],
        compiler_params=pltpu.CompilerParams(collective_id=collective_id, has_side_effects=True),
    )(flat)
    return summed.reshape(shape)


def per_device(
    sublevel_symbol_entries,
    prior_symbol_memory,
    entry_scaling_multiplier,
    entry_scaling_offset,
    learned_blending,
    blending_lowering_coefficients,
    blending_raising_coefficients,
    fading_lowering_coefficients,
    fading_raising_coefficients,
    learned_fading,
    immediate_item_premium,
    acceptor_projection,
    lookup_projection,
    payload_projection,
    gating_projection,
    emission_projection,
    group_scaling_multiplier,
    group_scaling_offset,
    dialogue_group_memory,
):
    rank = blending_raising_coefficients.shape[1]
    narrow_rows = dialogue_group_memory.shape[1]
    local_width = emission_projection.shape[1]
    group_partition = local_width // CHANNEL_SPAN
    sessions, steps, features = sublevel_symbol_entries.shape
    weights = (acceptor_projection, lookup_projection, payload_projection, gating_projection)

    floats = sublevel_symbol_entries.astype(jnp.float32)
    count = lax.axis_size("narrow")
    stats = narrow_sum(
        jnp.stack([jnp.sum(floats, -1), jnp.sum(floats * floats, -1)], 0), count, 0
    )
    center = stats[0][..., None] / FEATURE_EXTENT
    spread = stats[1][..., None] / FEATURE_EXTENT - center * center
    normed = (
        (floats - center) * lax.rsqrt(spread + 1e-05) * entry_scaling_multiplier
        + entry_scaling_offset
    ).astype(jnp.bfloat16)
    previous = jnp.concatenate([prior_symbol_memory[:, None], normed[:, :-1]], 1)
    normalized_float = normed.astype(jnp.float32)
    shifted_input = previous.astype(jnp.float32) - normalized_float
    blended = (normalized_float + shifted_input * learned_blending[0]).astype(jnp.bfloat16)
    partial_mix = jnp.einsum(
        "smd,dr->smr", blended, blending_lowering_coefficients,
        preferred_element_type=jnp.float32,
    )
    hidden_activation = jnp.tanh(narrow_sum(partial_mix, count, 1)).astype(jnp.bfloat16)
    decay_shift = jnp.einsum(
        "smr,rd->smd", hidden_activation[..., :rank], blending_raising_coefficients[0],
        preferred_element_type=jnp.float32,
    )
    decay_mix = (
        normalized_float + shifted_input * (learned_blending[1] + decay_shift)
    ).astype(jnp.bfloat16)
    partial_decay = jnp.einsum(
        "smd,dr->smr", decay_mix, fading_lowering_coefficients,
        preferred_element_type=jnp.float32,
    )
    decay_hidden = jnp.tanh(narrow_sum(partial_decay, count, 2)).astype(jnp.bfloat16)
    small = jnp.concatenate([hidden_activation[..., rank:], decay_hidden], -1)
    small_width = small.shape[-1]

    packed = jnp.concatenate(
        [prior_symbol_memory]
        + [normed[:, index] for index in range(steps)]
        + [small.reshape(sessions, steps * small_width)],
        -1,
    )
    packed_all = lax.all_gather(
        lax.all_gather(packed, "x", axis=0, tiled=True), "z", axis=0, tiled=True
    )
    small_start = (steps + 1) * features
    term_results = []
    for index in range(steps):
        previous_now = packed_all[:, index * features : (index + 1) * features]
        normed_now = packed_all[:, (index + 1) * features : (index + 2) * features]
        normalized_now = normed_now.astype(jnp.float32)
        shifted_now = previous_now.astype(jnp.float32) - normalized_now
        small_now = small_start + index * small_width
        for selector_index in range(4):
            low_rank_update = jnp.dot(
                packed_all[:, small_now + selector_index * rank : small_now + (selector_index + 1) * rank],
                blending_raising_coefficients[selector_index + 1],
                preferred_element_type=jnp.float32,
            )
            mixed_input = (
                normalized_now
                + shifted_now * (learned_blending[selector_index + 2] + low_rank_update)
            ).astype(jnp.bfloat16)
            term_results.append(
                jnp.dot(
                    mixed_input, weights[selector_index], preferred_element_type=jnp.float32
                ).astype(jnp.bfloat16)
            )
    projected = lax.psum_scatter(
        jnp.concatenate(term_results, -1), "narrow", scatter_dimension=0, tiled=True
    ).astype(jnp.float32).reshape(narrow_rows, steps, 4 * local_width)

    rows_start = lax.axis_index("narrow") * narrow_rows
    own_rows = lax.dynamic_slice_in_dim(packed_all[:, small_start:], rows_start, narrow_rows, 0)
    decay_rows = own_rows.reshape(narrow_rows, steps, small_width)[..., 4 * rank :]
    decay_log = learned_fading + jnp.einsum(
        "smr,rd->smd", decay_rows, fading_raising_coefficients,
        preferred_element_type=jnp.float32,
    )
    shrink_coefficient = jnp.exp(-jnp.exp(decay_log))

    def channel_set_first(block):
        return block.reshape(narrow_rows, group_partition, CHANNEL_SPAN).transpose(1, 2, 0)

    state = dialogue_group_memory.reshape(group_partition, CHANNEL_SPAN, CHANNEL_SPAN, narrow_rows)
    reward = immediate_item_premium.reshape(group_partition, CHANNEL_SPAN)
    pieces = []
    for index in range(steps):
        acceptor = channel_set_first(projected[:, index, :local_width])
        key_now = channel_set_first(projected[:, index, local_width : 2 * local_width])
        value_now = channel_set_first(projected[:, index, 2 * local_width : 3 * local_width])
        gate_now = projected[:, index, 3 * local_width :]
        forget_now = channel_set_first(shrink_coefficient[:, index])
        dyadic = key_now[:, :, None, :] * value_now[:, None, :, :]
        retrieval = jnp.sum(
            acceptor[:, :, None, :] * (state + reward[:, :, None, None] * dyadic), 1
        )
        state = forget_now[:, :, None, :] * state + dyadic
        center_r = jnp.mean(retrieval, 1, keepdims=True)
        offset = retrieval - center_r
        scaled = offset * lax.rsqrt(jnp.mean(offset * offset, 1, keepdims=True) + 0.00064)
        squashed = scaled.transpose(2, 0, 1).reshape(narrow_rows, local_width)
        pieces.append(
            (
                (squashed * group_scaling_multiplier + group_scaling_offset)
                * jax.nn.silu(gate_now)
            ).astype(jnp.bfloat16)
        )
    gated = jnp.stack(pieces, 1).reshape(narrow_rows * steps, local_width).T
    gated_all = lax.all_gather(
        lax.all_gather(gated, "x", axis=0, tiled=True), "z", axis=0, tiled=True
    )
    mixing_output = (
        jnp.einsum(
            "cs,ce->se", gated_all, emission_projection, preferred_element_type=jnp.float32
        )
        .astype(jnp.bfloat16)
        .reshape(narrow_rows, steps, local_width)
    )
    return (
        mixing_output,
        state.reshape(group_partition * CHANNEL_SPAN * CHANNEL_SPAN, narrow_rows),
    )


def solution(mesh):
    wide_size = mesh.shape["wide"]
    x_size = 4 if wide_size % 4 == 0 else 1
    split = jax.sharding.Mesh(
        mesh.devices.reshape(wide_size // x_size, x_size, mesh.shape["narrow"]),
        ("z", "x", "narrow"),
    )
    wide = ("z", "x")
    placed = (
        P(wide, None, "narrow"),
        P(wide, "narrow"),
        P("narrow"),
        P("narrow"),
        P(None, "narrow"),
        P("narrow", None),
        P(None, None, "narrow"),
        P("narrow", None),
        P(None, wide),
        P(wide),
        P(wide),
        P("narrow", wide),
        P("narrow", wide),
        P("narrow", wide),
        P("narrow", wide),
        P(None, wide),
        P(wide),
        P(wide),
        P(wide, "narrow"),
    )
    return jax.shard_map(
        per_device,
        mesh=split,
        in_specs=placed,
        out_specs=(P("narrow", None, wide), P(wide, "narrow")),
        check_vma=False,
    )
```

```python
import jax
import jax.numpy as jnp
from jax import lax
from jax.sharding import PartitionSpec as P
from jax.experimental import pallas as pl
from jax.experimental.pallas import tpu as pltpu

CHANNEL_SPAN = 64
FEATURE_EXTENT = 4096


def narrow_sum_kernel(count, x_ref, o_ref, recv, send_sems, recv_sems):
    me = lax.axis_index("narrow")
    here = (lax.axis_index("z"), lax.axis_index("x"))

    def peer_id(peer):
        return here + (peer,)

    barrier = pltpu.get_barrier_semaphore()
    for peer in range(count):
        @pl.when(peer != me)
        def _():
            pl.semaphore_signal(
                barrier, 1, device_id=peer_id(peer), device_id_type=pl.DeviceIdType.MESH
            )
    pl.semaphore_wait(barrier, count - 1)

    def outgoing(peer):
        return pltpu.make_async_remote_copy(
            src_ref=x_ref,
            dst_ref=recv.at[me],
            send_sem=send_sems.at[peer],
            recv_sem=recv_sems.at[me],
            device_id=peer_id(peer),
            device_id_type=pl.DeviceIdType.MESH,
        )

    def incoming(peer):
        return pltpu.make_async_remote_copy(
            src_ref=x_ref,
            dst_ref=recv.at[peer],
            send_sem=send_sems.at[peer],
            recv_sem=recv_sems.at[peer],
            device_id=peer_id(peer),
            device_id_type=pl.DeviceIdType.MESH,
        )

    for peer in range(count):
        @pl.when(peer != me)
        def _():
            outgoing(peer).start()

    recv[me] = x_ref[...]
    for peer in range(count):
        @pl.when(peer != me)
        def _():
            outgoing(peer).wait_send()
            incoming(peer).wait_recv()

    total = recv[0]
    for peer in range(1, count):
        total = total + recv[peer]
    o_ref[...] = total


def narrow_sum(value, count, collective_id):
    shape = value.shape
    flat = value.reshape(-1, 128)
    summed = pl.pallas_call(
        lambda *refs: narrow_sum_kernel(count, *refs),
        out_shape=jax.ShapeDtypeStruct(flat.shape, flat.dtype),
        in_specs=[pl.BlockSpec(memory_space=pltpu.VMEM)],
        out_specs=pl.BlockSpec(memory_space=pltpu.VMEM),
        scratch_shapes=[
            pltpu.VMEM((count,) + flat.shape, flat.dtype),
            pltpu.SemaphoreType.DMA((count,)),
            pltpu.SemaphoreType.DMA((count,)),
        ],
        compiler_params=pltpu.CompilerParams(collective_id=collective_id, has_side_effects=True),
    )(flat)
    return summed.reshape(shape)


def z_gather_kernel(size, x_ref, o_ref, buf, send_right, send_left, recv_sems):
    me = lax.axis_index("z")
    right = lax.rem(me + 1, size)
    left = lax.rem(me + size - 1, size)

    def device(position):
        return (position, lax.axis_index("x"), lax.axis_index("narrow"))

    barrier = pltpu.get_barrier_semaphore()
    for neighbour in (left, right):
        pl.semaphore_signal(
            barrier, 1, device_id=device(neighbour), device_id_type=pl.DeviceIdType.MESH
        )
    pl.semaphore_wait(barrier, 2)

    def send(source, origin, sem, target):
        copy = pltpu.make_async_remote_copy(
            src_ref=source,
            dst_ref=buf.at[origin],
            send_sem=sem,
            recv_sem=recv_sems.at[origin],
            device_id=device(target),
            device_id_type=pl.DeviceIdType.MESH,
        )
        copy.start()
        return copy

    def arrived(origin):
        pltpu.make_async_remote_copy(
            src_ref=buf.at[origin],
            dst_ref=buf.at[origin],
            send_sem=send_right.at[0],
            recv_sem=recv_sems.at[origin],
            device_id=device(right),
            device_id_type=pl.DeviceIdType.MESH,
        ).wait_recv()

    rightward = size // 2
    leftward = size - 1 - rightward
    sends = []
    for step in range(rightward):
        origin = lax.rem(me - step + size, size)
        if step > 0:
            arrived(origin)
        source = x_ref if step == 0 else buf.at[origin]
        sends.append(send(source, origin, send_right.at[step], right))
        if step < leftward:
            origin = lax.rem(me + step, size)
            if step > 0:
                arrived(origin)
            source = x_ref if step == 0 else buf.at[origin]
            sends.append(send(source, origin, send_left.at[step], left))
    arrived(lax.rem(me - rightward + size, size))
    if leftward > 0:
        arrived(lax.rem(me + leftward, size))
    for copy in sends:
        copy.wait_send()
    buf[me] = x_ref[...]
    o_ref[...] = buf[...]


def z_gather(value, size, collective_id):
    rightward = size // 2
    leftward = max(size - 1 - rightward, 1)
    gathered = pl.pallas_call(
        lambda *refs: z_gather_kernel(size, *refs),
        out_shape=jax.ShapeDtypeStruct((size,) + value.shape, value.dtype),
        in_specs=[pl.BlockSpec(memory_space=pltpu.VMEM)],
        out_specs=pl.BlockSpec(memory_space=pltpu.VMEM),
        scratch_shapes=[
            pltpu.VMEM((size,) + value.shape, value.dtype),
            pltpu.SemaphoreType.DMA((rightward,)),
            pltpu.SemaphoreType.DMA((leftward,)),
            pltpu.SemaphoreType.DMA((size,)),
        ],
        compiler_params=pltpu.CompilerParams(collective_id=collective_id, has_side_effects=True),
    )(value)
    return gathered.reshape((size * value.shape[0],) + value.shape[1:])


def per_device(
    sublevel_symbol_entries,
    prior_symbol_memory,
    entry_scaling_multiplier,
    entry_scaling_offset,
    learned_blending,
    blending_lowering_coefficients,
    blending_raising_coefficients,
    fading_lowering_coefficients,
    fading_raising_coefficients,
    learned_fading,
    immediate_item_premium,
    acceptor_projection,
    lookup_projection,
    payload_projection,
    gating_projection,
    emission_projection,
    group_scaling_multiplier,
    group_scaling_offset,
    dialogue_group_memory,
):
    rank = blending_raising_coefficients.shape[1]
    narrow_rows = dialogue_group_memory.shape[1]
    local_width = emission_projection.shape[1]
    group_partition = local_width // CHANNEL_SPAN
    sessions, steps, features = sublevel_symbol_entries.shape
    weights = (acceptor_projection, lookup_projection, payload_projection, gating_projection)

    floats = sublevel_symbol_entries.astype(jnp.float32)
    count = lax.axis_size("narrow")
    stats = narrow_sum(
        jnp.stack([jnp.sum(floats, -1), jnp.sum(floats * floats, -1)], 0), count, 0
    )
    center = stats[0][..., None] / FEATURE_EXTENT
    spread = stats[1][..., None] / FEATURE_EXTENT - center * center
    normed = (
        (floats - center) * lax.rsqrt(spread + 1e-05) * entry_scaling_multiplier
        + entry_scaling_offset
    ).astype(jnp.bfloat16)
    previous = jnp.concatenate([prior_symbol_memory[:, None], normed[:, :-1]], 1)
    normalized_float = normed.astype(jnp.float32)
    shifted_input = previous.astype(jnp.float32) - normalized_float
    blended = (normalized_float + shifted_input * learned_blending[0]).astype(jnp.bfloat16)
    partial_mix = jnp.einsum(
        "smd,dr->smr", blended, blending_lowering_coefficients,
        preferred_element_type=jnp.float32,
    )
    hidden_activation = jnp.tanh(narrow_sum(partial_mix, count, 1)).astype(jnp.bfloat16)
    decay_shift = jnp.einsum(
        "smr,rd->smd", hidden_activation[..., :rank], blending_raising_coefficients[0],
        preferred_element_type=jnp.float32,
    )
    decay_mix = (
        normalized_float + shifted_input * (learned_blending[1] + decay_shift)
    ).astype(jnp.bfloat16)
    partial_decay = jnp.einsum(
        "smd,dr->smr", decay_mix, fading_lowering_coefficients,
        preferred_element_type=jnp.float32,
    )
    decay_hidden = jnp.tanh(narrow_sum(partial_decay, count, 2)).astype(jnp.bfloat16)
    small = jnp.concatenate([hidden_activation[..., rank:], decay_hidden], -1)
    small_width = small.shape[-1]

    packed = jnp.concatenate(
        [prior_symbol_memory]
        + [normed[:, index] for index in range(steps)]
        + [small.reshape(sessions, steps * small_width)],
        -1,
    )
    z_size = lax.axis_size("z")
    packed_all = z_gather(lax.all_gather(packed, "x", axis=0, tiled=True), z_size, 3)
    small_start = (steps + 1) * features
    term_results = []
    for index in range(steps):
        previous_now = packed_all[:, index * features : (index + 1) * features]
        normed_now = packed_all[:, (index + 1) * features : (index + 2) * features]
        normalized_now = normed_now.astype(jnp.float32)
        shifted_now = previous_now.astype(jnp.float32) - normalized_now
        small_now = small_start + index * small_width
        for selector_index in range(4):
            low_rank_update = jnp.dot(
                packed_all[:, small_now + selector_index * rank : small_now + (selector_index + 1) * rank],
                blending_raising_coefficients[selector_index + 1],
                preferred_element_type=jnp.float32,
            )
            mixed_input = (
                normalized_now
                + shifted_now * (learned_blending[selector_index + 2] + low_rank_update)
            ).astype(jnp.bfloat16)
            term_results.append(
                jnp.dot(
                    mixed_input, weights[selector_index], preferred_element_type=jnp.float32
                ).astype(jnp.bfloat16)
            )
    projected = lax.psum_scatter(
        jnp.concatenate(term_results, -1), "narrow", scatter_dimension=0, tiled=True
    ).astype(jnp.float32).reshape(narrow_rows, steps, 4 * local_width)

    rows_start = lax.axis_index("narrow") * narrow_rows
    own_rows = lax.dynamic_slice_in_dim(packed_all[:, small_start:], rows_start, narrow_rows, 0)
    decay_rows = own_rows.reshape(narrow_rows, steps, small_width)[..., 4 * rank :]
    decay_log = learned_fading + jnp.einsum(
        "smr,rd->smd", decay_rows, fading_raising_coefficients,
        preferred_element_type=jnp.float32,
    )
    shrink_coefficient = jnp.exp(-jnp.exp(decay_log))

    def channel_set_first(block):
        return block.reshape(narrow_rows, group_partition, CHANNEL_SPAN).transpose(1, 2, 0)

    state = dialogue_group_memory.reshape(group_partition, CHANNEL_SPAN, CHANNEL_SPAN, narrow_rows)
    reward = immediate_item_premium.reshape(group_partition, CHANNEL_SPAN)
    pieces = []
    for index in range(steps):
        acceptor = channel_set_first(projected[:, index, :local_width])
        key_now = channel_set_first(projected[:, index, local_width : 2 * local_width])
        value_now = channel_set_first(projected[:, index, 2 * local_width : 3 * local_width])
        gate_now = projected[:, index, 3 * local_width :]
        forget_now = channel_set_first(shrink_coefficient[:, index])
        dyadic = key_now[:, :, None, :] * value_now[:, None, :, :]
        retrieval = jnp.sum(
            acceptor[:, :, None, :] * (state + reward[:, :, None, None] * dyadic), 1
        )
        state = forget_now[:, :, None, :] * state + dyadic
        center_r = jnp.mean(retrieval, 1, keepdims=True)
        offset = retrieval - center_r
        scaled = offset * lax.rsqrt(jnp.mean(offset * offset, 1, keepdims=True) + 0.00064)
        squashed = scaled.transpose(2, 0, 1).reshape(narrow_rows, local_width)
        pieces.append(
            (
                (squashed * group_scaling_multiplier + group_scaling_offset)
                * jax.nn.silu(gate_now)
            ).astype(jnp.bfloat16)
        )
    gated = jnp.stack(pieces, 1).reshape(narrow_rows * steps, local_width).T
    gated_all = z_gather(lax.all_gather(gated, "x", axis=0, tiled=True), z_size, 4)
    mixing_output = (
        jnp.einsum(
            "cs,ce->se", gated_all, emission_projection, preferred_element_type=jnp.float32
        )
        .astype(jnp.bfloat16)
        .reshape(narrow_rows, steps, local_width)
    )
    return (
        mixing_output,
        state.reshape(group_partition * CHANNEL_SPAN * CHANNEL_SPAN, narrow_rows),
    )


def solution(mesh):
    wide_size = mesh.shape["wide"]
    x_size = 4 if wide_size % 4 == 0 else 1
    split = jax.sharding.Mesh(
        mesh.devices.reshape(wide_size // x_size, x_size, mesh.shape["narrow"]),
        ("z", "x", "narrow"),
    )
    wide = ("z", "x")
    placed = (
        P(wide, None, "narrow"),
        P(wide, "narrow"),
        P("narrow"),
        P("narrow"),
        P(None, "narrow"),
        P("narrow", None),
        P(None, None, "narrow"),
        P("narrow", None),
        P(None, wide),
        P(wide),
        P(wide),
        P("narrow", wide),
        P("narrow", wide),
        P("narrow", wide),
        P("narrow", wide),
        P(None, wide),
        P(wide),
        P(wide),
        P(wide, "narrow"),
    )
    return jax.shard_map(
        per_device,
        mesh=split,
        in_specs=placed,
        out_specs=(P("narrow", None, wide), P(wide, "narrow")),
        check_vma=False,
    )
```

```python
import jax
import jax.numpy as jnp
from jax import lax
from jax.sharding import PartitionSpec as P
from jax.experimental import pallas as pl
from jax.experimental.pallas import tpu as pltpu

CHANNEL_SPAN = 64
FEATURE_EXTENT = 4096


def narrow_sum_kernel(count, x_ref, o_ref, recv, send_sems, recv_sems):
    me = lax.axis_index("narrow")
    here = (lax.axis_index("z"), lax.axis_index("x"))

    def peer_id(peer):
        return here + (peer,)

    barrier = pltpu.get_barrier_semaphore()
    for peer in range(count):
        @pl.when(peer != me)
        def _():
            pl.semaphore_signal(
                barrier, 1, device_id=peer_id(peer), device_id_type=pl.DeviceIdType.MESH
            )
    pl.semaphore_wait(barrier, count - 1)

    def outgoing(peer):
        return pltpu.make_async_remote_copy(
            src_ref=x_ref,
            dst_ref=recv.at[me],
            send_sem=send_sems.at[peer],
            recv_sem=recv_sems.at[me],
            device_id=peer_id(peer),
            device_id_type=pl.DeviceIdType.MESH,
        )

    def incoming(peer):
        return pltpu.make_async_remote_copy(
            src_ref=x_ref,
            dst_ref=recv.at[peer],
            send_sem=send_sems.at[peer],
            recv_sem=recv_sems.at[peer],
            device_id=peer_id(peer),
            device_id_type=pl.DeviceIdType.MESH,
        )

    for peer in range(count):
        @pl.when(peer != me)
        def _():
            outgoing(peer).start()

    recv[me] = x_ref[...]
    for peer in range(count):
        @pl.when(peer != me)
        def _():
            outgoing(peer).wait_send()
            incoming(peer).wait_recv()

    total = recv[0]
    for peer in range(1, count):
        total = total + recv[peer]
    o_ref[...] = total


def narrow_sum(value, count, collective_id):
    shape = value.shape
    flat = value.reshape(-1, 128)
    summed = pl.pallas_call(
        lambda *refs: narrow_sum_kernel(count, *refs),
        out_shape=jax.ShapeDtypeStruct(flat.shape, flat.dtype),
        in_specs=[pl.BlockSpec(memory_space=pltpu.VMEM)],
        out_specs=pl.BlockSpec(memory_space=pltpu.VMEM),
        scratch_shapes=[
            pltpu.VMEM((count,) + flat.shape, flat.dtype),
            pltpu.SemaphoreType.DMA((count,)),
            pltpu.SemaphoreType.DMA((count,)),
        ],
        compiler_params=pltpu.CompilerParams(collective_id=collective_id, has_side_effects=True),
    )(flat)
    return summed.reshape(shape)


def z_gather_kernel(size, x_ref, o_ref, buf, send_right, send_left, recv_sems):
    me = lax.axis_index("z")
    right = lax.rem(me + 1, size)
    left = lax.rem(me + size - 1, size)

    def device(position):
        return (position, lax.axis_index("x"), lax.axis_index("narrow"))

    barrier = pltpu.get_barrier_semaphore()
    for neighbour in (left, right):
        pl.semaphore_signal(
            barrier, 1, device_id=device(neighbour), device_id_type=pl.DeviceIdType.MESH
        )
    pl.semaphore_wait(barrier, 2)

    def send(source, origin, sem, target):
        copy = pltpu.make_async_remote_copy(
            src_ref=source,
            dst_ref=buf.at[origin],
            send_sem=sem,
            recv_sem=recv_sems.at[origin],
            device_id=device(target),
            device_id_type=pl.DeviceIdType.MESH,
        )
        copy.start()
        return copy

    def arrived(origin):
        pltpu.make_async_remote_copy(
            src_ref=buf.at[origin],
            dst_ref=buf.at[origin],
            send_sem=send_right.at[0],
            recv_sem=recv_sems.at[origin],
            device_id=device(right),
            device_id_type=pl.DeviceIdType.MESH,
        ).wait_recv()

    rightward = size // 2
    leftward = size - 1 - rightward
    sends = []
    for step in range(rightward):
        origin = lax.rem(me - step + size, size)
        if step > 0:
            arrived(origin)
        source = x_ref if step == 0 else buf.at[origin]
        sends.append(send(source, origin, send_right.at[step], right))
        if step < leftward:
            origin = lax.rem(me + step, size)
            if step > 0:
                arrived(origin)
            source = x_ref if step == 0 else buf.at[origin]
            sends.append(send(source, origin, send_left.at[step], left))
    arrived(lax.rem(me - rightward + size, size))
    if leftward > 0:
        arrived(lax.rem(me + leftward, size))
    for copy in sends:
        copy.wait_send()
    buf[me] = x_ref[...]
    o_ref[...] = buf[...]


def z_gather(value, size, collective_id):
    rightward = size // 2
    leftward = max(size - 1 - rightward, 1)
    gathered = pl.pallas_call(
        lambda *refs: z_gather_kernel(size, *refs),
        out_shape=jax.ShapeDtypeStruct((size,) + value.shape, value.dtype),
        in_specs=[pl.BlockSpec(memory_space=pltpu.VMEM)],
        out_specs=pl.BlockSpec(memory_space=pltpu.VMEM),
        scratch_shapes=[
            pltpu.VMEM((size,) + value.shape, value.dtype),
            pltpu.SemaphoreType.DMA((rightward,)),
            pltpu.SemaphoreType.DMA((leftward,)),
            pltpu.SemaphoreType.DMA((size,)),
        ],
        compiler_params=pltpu.CompilerParams(collective_id=collective_id, has_side_effects=True),
    )(value)
    return gathered.reshape((size * value.shape[0],) + value.shape[1:])


def z_project_kernel(size, steps, features, x_ref, mix_ref, blend_ref, w_ref,
                     decay_ref, terms_ref, buf, send_right, send_left, recv_sems):
    me = lax.axis_index("z")
    right = lax.rem(me + 1, size)
    left = lax.rem(me + size - 1, size)
    hidden_start = (steps + 1) * features
    hidden_width = mix_ref.shape[1]
    decay_start = hidden_start + steps * hidden_width

    def device(position):
        return (position, lax.axis_index("x"), lax.axis_index("narrow"))

    barrier = pltpu.get_barrier_semaphore()
    for neighbour in (left, right):
        pl.semaphore_signal(
            barrier, 1, device_id=device(neighbour), device_id_type=pl.DeviceIdType.MESH
        )
    pl.semaphore_wait(barrier, 2)

    def send(source, origin, sem, target):
        copy = pltpu.make_async_remote_copy(
            src_ref=source,
            dst_ref=buf.at[origin],
            send_sem=sem,
            recv_sem=recv_sems.at[origin],
            device_id=device(target),
            device_id_type=pl.DeviceIdType.MESH,
        )
        copy.start()
        return copy

    def arrived(origin):
        pltpu.make_async_remote_copy(
            src_ref=buf.at[origin],
            dst_ref=buf.at[origin],
            send_sem=send_right.at[0],
            recv_sem=recv_sems.at[origin],
            device_id=device(right),
            device_id_type=pl.DeviceIdType.MESH,
        ).wait_recv()

    def project(block, origin):
        selectors = w_ref.shape[0]
        for index in range(steps):
            previous = block[:, index * features : (index + 1) * features].astype(jnp.float32)
            normed = block[:, (index + 1) * features : (index + 2) * features].astype(jnp.float32)
            shifted = previous - normed
            hidden = block[:, hidden_start + index * hidden_width : hidden_start + (index + 1) * hidden_width]
            for selector in range(selectors):
                low_rank = jnp.dot(hidden, mix_ref[selector], preferred_element_type=jnp.float32)
                mixed = (
                    normed + shifted * (blend_ref[selector + 2 : selector + 3, :] + low_rank)
                ).astype(jnp.bfloat16)
                terms_ref[origin, index * selectors + selector] = jnp.dot(
                    mixed, w_ref[selector], preferred_element_type=jnp.float32
                ).astype(terms_ref.dtype)

    rightward = size // 2
    leftward = size - 1 - rightward
    sends = []
    for step in range(rightward):
        origin = lax.rem(me - step + size, size)
        if step > 0:
            arrived(origin)
        source = x_ref if step == 0 else buf.at[origin]
        sends.append(send(source, origin, send_right.at[step], right))
        if step < leftward:
            other = lax.rem(me + step, size)
            if step > 0:
                arrived(other)
                sends.append(send(buf.at[other], other, send_left.at[step], left))
            else:
                sends.append(send(x_ref, other, send_left.at[step], left))
        project(source, origin)
        if 0 < step < leftward:
            project(buf.at[other], other)
    last_right = lax.rem(me - rightward + size, size)
    arrived(last_right)
    project(buf.at[last_right], last_right)
    if leftward > 0:
        last_left = lax.rem(me + leftward, size)
        arrived(last_left)
        project(buf.at[last_left], last_left)
    for copy in sends:
        copy.wait_send()
    buf[me] = x_ref[...]
    decay_ref[...] = buf[:, :, decay_start:]


def z_project(value, mix, blend, stacked, size, steps, features, collective_id):
    rightward = size // 2
    leftward = max(size - 1 - rightward, 1)
    rows, width = value.shape
    selectors, _, out_width = stacked.shape
    decay_start = (steps + 1) * features + steps * mix.shape[1]
    return pl.pallas_call(
        lambda *refs: z_project_kernel(size, steps, features, *refs),
        out_shape=(
            jax.ShapeDtypeStruct((size, rows, width - decay_start), value.dtype),
            jax.ShapeDtypeStruct((size, steps * selectors, rows, out_width), jnp.bfloat16),
        ),
        in_specs=[pl.BlockSpec(memory_space=pltpu.VMEM)] * 4,
        out_specs=(pl.BlockSpec(memory_space=pltpu.VMEM), pl.BlockSpec(memory_space=pltpu.VMEM)),
        scratch_shapes=[
            pltpu.VMEM((size, rows, width), value.dtype),
            pltpu.SemaphoreType.DMA((rightward,)),
            pltpu.SemaphoreType.DMA((leftward,)),
            pltpu.SemaphoreType.DMA((size,)),
        ],
        compiler_params=pltpu.CompilerParams(collective_id=collective_id, has_side_effects=True),
    )(value, mix, blend, stacked)


def per_device(
    sublevel_symbol_entries,
    prior_symbol_memory,
    entry_scaling_multiplier,
    entry_scaling_offset,
    learned_blending,
    blending_lowering_coefficients,
    blending_raising_coefficients,
    fading_lowering_coefficients,
    fading_raising_coefficients,
    learned_fading,
    immediate_item_premium,
    acceptor_projection,
    lookup_projection,
    payload_projection,
    gating_projection,
    emission_projection,
    group_scaling_multiplier,
    group_scaling_offset,
    dialogue_group_memory,
):
    rank = blending_raising_coefficients.shape[1]
    narrow_rows = dialogue_group_memory.shape[1]
    local_width = emission_projection.shape[1]
    group_partition = local_width // CHANNEL_SPAN
    sessions, steps, features = sublevel_symbol_entries.shape
    weights = (acceptor_projection, lookup_projection, payload_projection, gating_projection)

    floats = sublevel_symbol_entries.astype(jnp.float32)
    count = lax.axis_size("narrow")
    stats = narrow_sum(
        jnp.stack([jnp.sum(floats, -1), jnp.sum(floats * floats, -1)], 0), count, 0
    )
    center = stats[0][..., None] / FEATURE_EXTENT
    spread = stats[1][..., None] / FEATURE_EXTENT - center * center
    normed = (
        (floats - center) * lax.rsqrt(spread + 1e-05) * entry_scaling_multiplier
        + entry_scaling_offset
    ).astype(jnp.bfloat16)
    previous = jnp.concatenate([prior_symbol_memory[:, None], normed[:, :-1]], 1)
    normalized_float = normed.astype(jnp.float32)
    shifted_input = previous.astype(jnp.float32) - normalized_float
    blended = (normalized_float + shifted_input * learned_blending[0]).astype(jnp.bfloat16)
    partial_mix = jnp.einsum(
        "smd,dr->smr", blended, blending_lowering_coefficients,
        preferred_element_type=jnp.float32,
    )
    hidden_activation = jnp.tanh(narrow_sum(partial_mix, count, 1)).astype(jnp.bfloat16)
    decay_shift = jnp.einsum(
        "smr,rd->smd", hidden_activation[..., :rank], blending_raising_coefficients[0],
        preferred_element_type=jnp.float32,
    )
    decay_mix = (
        normalized_float + shifted_input * (learned_blending[1] + decay_shift)
    ).astype(jnp.bfloat16)
    partial_decay = jnp.einsum(
        "smd,dr->smr", decay_mix, fading_lowering_coefficients,
        preferred_element_type=jnp.float32,
    )
    decay_hidden = jnp.tanh(narrow_sum(partial_decay, count, 2)).astype(jnp.bfloat16)
    hidden_width = hidden_activation.shape[-1] - rank
    decay_width = decay_hidden.shape[-1]
    packed = jnp.concatenate(
        [prior_symbol_memory]
        + [normed[:, index] for index in range(steps)]
        + [
            hidden_activation[..., rank:].reshape(sessions, steps * hidden_width),
            decay_hidden.reshape(sessions, steps * decay_width),
        ],
        -1,
    )
    selectors = len(weights)
    mask = jnp.eye(selectors, dtype=blending_raising_coefficients.dtype)
    mix_stack = jnp.einsum(
        "ij,jrd->ijrd", mask, blending_raising_coefficients[1 : selectors + 1]
    ).reshape(selectors, selectors * rank, features)
    z_size = lax.axis_size("z")
    decay_all, terms = z_project(
        lax.all_gather(packed, "x", axis=0, tiled=True),
        mix_stack,
        learned_blending,
        jnp.stack(weights, 0),
        z_size,
        steps,
        features,
        3,
    )
    slots_per_device = z_size // lax.axis_size("narrow")
    projected = lax.psum_scatter(terms, "narrow", scatter_dimension=0, tiled=True)
    slot_rows = terms.shape[2]
    projected = (
        projected.reshape(slots_per_device, steps, selectors, slot_rows, local_width)
        .transpose(0, 3, 1, 2, 4)
        .reshape(narrow_rows, steps, selectors * local_width)
        .astype(jnp.float32)
    )

    rows_start = lax.axis_index("narrow") * narrow_rows
    own_rows = lax.dynamic_slice_in_dim(
        decay_all.reshape(-1, decay_all.shape[-1]), rows_start, narrow_rows, 0
    )
    decay_rows = own_rows.reshape(narrow_rows, steps, decay_width)
    decay_log = learned_fading + jnp.einsum(
        "smr,rd->smd", decay_rows, fading_raising_coefficients,
        preferred_element_type=jnp.float32,
    )
    shrink_coefficient = jnp.exp(-jnp.exp(decay_log))

    def channel_set_first(block):
        return block.reshape(narrow_rows, group_partition, CHANNEL_SPAN).transpose(1, 2, 0)

    state = dialogue_group_memory.reshape(group_partition, CHANNEL_SPAN, CHANNEL_SPAN, narrow_rows)
    reward = immediate_item_premium.reshape(group_partition, CHANNEL_SPAN)
    pieces = []
    for index in range(steps):
        acceptor = channel_set_first(projected[:, index, :local_width])
        key_now = channel_set_first(projected[:, index, local_width : 2 * local_width])
        value_now = channel_set_first(projected[:, index, 2 * local_width : 3 * local_width])
        gate_now = projected[:, index, 3 * local_width :]
        forget_now = channel_set_first(shrink_coefficient[:, index])
        dyadic = key_now[:, :, None, :] * value_now[:, None, :, :]
        retrieval = jnp.sum(
            acceptor[:, :, None, :] * (state + reward[:, :, None, None] * dyadic), 1
        )
        state = forget_now[:, :, None, :] * state + dyadic
        center_r = jnp.mean(retrieval, 1, keepdims=True)
        offset = retrieval - center_r
        scaled = offset * lax.rsqrt(jnp.mean(offset * offset, 1, keepdims=True) + 0.00064)
        squashed = scaled.transpose(2, 0, 1).reshape(narrow_rows, local_width)
        pieces.append(
            (
                (squashed * group_scaling_multiplier + group_scaling_offset)
                * jax.nn.silu(gate_now)
            ).astype(jnp.bfloat16)
        )
    gated = jnp.stack(pieces, 1).reshape(narrow_rows * steps, local_width).T
    gated_all = z_gather(lax.all_gather(gated, "x", axis=0, tiled=True), z_size, 4)
    mixing_output = (
        jnp.einsum(
            "cs,ce->se", gated_all, emission_projection, preferred_element_type=jnp.float32
        )
        .astype(jnp.bfloat16)
        .reshape(narrow_rows, steps, local_width)
    )
    return (
        mixing_output,
        state.reshape(group_partition * CHANNEL_SPAN * CHANNEL_SPAN, narrow_rows),
    )


def solution(mesh):
    wide_size = mesh.shape["wide"]
    x_size = 4 if wide_size % 4 == 0 else 1
    split = jax.sharding.Mesh(
        mesh.devices.reshape(wide_size // x_size, x_size, mesh.shape["narrow"]),
        ("z", "x", "narrow"),
    )
    wide = ("z", "x")
    placed = (
        P(wide, None, "narrow"),
        P(wide, "narrow"),
        P("narrow"),
        P("narrow"),
        P(None, "narrow"),
        P("narrow", None),
        P(None, None, "narrow"),
        P("narrow", None),
        P(None, wide),
        P(wide),
        P(wide),
        P("narrow", wide),
        P("narrow", wide),
        P("narrow", wide),
        P("narrow", wide),
        P(None, wide),
        P(wide),
        P(wide),
        P(wide, "narrow"),
    )
    return jax.shard_map(
        per_device,
        mesh=split,
        in_specs=placed,
        out_specs=(P("narrow", None, wide), P(wide, "narrow")),
        check_vma=False,
    )
```

```python
import jax
import jax.numpy as jnp
from jax import lax
from jax.sharding import PartitionSpec as P
from jax.experimental import pallas as pl
from jax.experimental.pallas import tpu as pltpu

CHANNEL_SPAN = 64
FEATURE_EXTENT = 4096


def narrow_sum_kernel(count, x_ref, o_ref, recv, send_sems, recv_sems):
    me = lax.axis_index("narrow")
    here = (lax.axis_index("z"), lax.axis_index("x"))

    def peer_id(peer):
        return here + (peer,)

    barrier = pltpu.get_barrier_semaphore()
    for peer in range(count):
        @pl.when(peer != me)
        def _():
            pl.semaphore_signal(
                barrier, 1, device_id=peer_id(peer), device_id_type=pl.DeviceIdType.MESH
            )
    pl.semaphore_wait(barrier, count - 1)

    def outgoing(peer):
        return pltpu.make_async_remote_copy(
            src_ref=x_ref,
            dst_ref=recv.at[me],
            send_sem=send_sems.at[peer],
            recv_sem=recv_sems.at[me],
            device_id=peer_id(peer),
            device_id_type=pl.DeviceIdType.MESH,
        )

    def incoming(peer):
        return pltpu.make_async_remote_copy(
            src_ref=x_ref,
            dst_ref=recv.at[peer],
            send_sem=send_sems.at[peer],
            recv_sem=recv_sems.at[peer],
            device_id=peer_id(peer),
            device_id_type=pl.DeviceIdType.MESH,
        )

    for peer in range(count):
        @pl.when(peer != me)
        def _():
            outgoing(peer).start()

    recv[me] = x_ref[...]
    for peer in range(count):
        @pl.when(peer != me)
        def _():
            outgoing(peer).wait_send()
            incoming(peer).wait_recv()

    total = recv[0]
    for peer in range(1, count):
        total = total + recv[peer]
    o_ref[...] = total


def narrow_sum(value, count, collective_id):
    shape = value.shape
    flat = value.reshape(-1, 128)
    summed = pl.pallas_call(
        lambda *refs: narrow_sum_kernel(count, *refs),
        out_shape=jax.ShapeDtypeStruct(flat.shape, flat.dtype),
        in_specs=[pl.BlockSpec(memory_space=pltpu.VMEM)],
        out_specs=pl.BlockSpec(memory_space=pltpu.VMEM),
        scratch_shapes=[
            pltpu.VMEM((count,) + flat.shape, flat.dtype),
            pltpu.SemaphoreType.DMA((count,)),
            pltpu.SemaphoreType.DMA((count,)),
        ],
        compiler_params=pltpu.CompilerParams(collective_id=collective_id, has_side_effects=True),
    )(flat)
    return summed.reshape(shape)


def gather_row(x_ref, buf, x_sems, local_sem, send_x, device, me, x_size):
    mine = lax.axis_index("x")
    rows = x_ref.shape[0]
    local = pltpu.make_async_copy(x_ref, buf.at[me, pl.ds(mine * rows, rows)], local_sem)
    local.start()
    sends = []
    for peer in range(x_size):
        @pl.when(peer != mine)
        def _():
            pltpu.make_async_remote_copy(
                src_ref=x_ref,
                dst_ref=buf.at[me, pl.ds(mine * rows, rows)],
                send_sem=send_x.at[peer],
                recv_sem=x_sems.at[mine],
                device_id=device(me, peer),
                device_id_type=pl.DeviceIdType.MESH,
            ).start()
    local.wait()
    for peer in range(x_size):
        @pl.when(peer != mine)
        def _():
            pltpu.make_async_remote_copy(
                src_ref=x_ref,
                dst_ref=buf.at[me, pl.ds(peer * rows, rows)],
                send_sem=send_x.at[peer],
                recv_sem=x_sems.at[peer],
                device_id=device(me, peer),
                device_id_type=pl.DeviceIdType.MESH,
            ).wait_recv()

    def finish():
        for peer in range(x_size):
            @pl.when(peer != mine)
            def _():
                pltpu.make_async_remote_copy(
                    src_ref=x_ref,
                    dst_ref=buf.at[me, pl.ds(mine * rows, rows)],
                    send_sem=send_x.at[peer],
                    recv_sem=x_sems.at[mine],
                    device_id=device(me, peer),
                    device_id_type=pl.DeviceIdType.MESH,
                ).wait_send()

    return finish


def greet(device, me, left, right, x_size):
    mine = lax.axis_index("x")
    barrier = pltpu.get_barrier_semaphore()
    for neighbour in (left, right):
        pl.semaphore_signal(
            barrier, 1, device_id=device(neighbour, mine), device_id_type=pl.DeviceIdType.MESH
        )
    for peer in range(x_size):
        @pl.when(peer != mine)
        def _():
            pl.semaphore_signal(
                barrier, 1, device_id=device(me, peer), device_id_type=pl.DeviceIdType.MESH
            )
    pl.semaphore_wait(barrier, 2 + x_size - 1)


def z_gather_kernel(size, x_size, x_ref, o_ref, buf, send_right, send_left, recv_sems,
                    x_sems, local_sem, send_x):
    me = lax.axis_index("z")
    right = lax.rem(me + 1, size)
    left = lax.rem(me + size - 1, size)

    def device(position, column=None):
        column = lax.axis_index("x") if column is None else column
        return (position, column, lax.axis_index("narrow"))

    greet(device, me, left, right, x_size)
    finish_row = gather_row(x_ref, buf, x_sems, local_sem, send_x, device, me, x_size)

    def send(source, origin, sem, target):
        copy = pltpu.make_async_remote_copy(
            src_ref=source,
            dst_ref=buf.at[origin],
            send_sem=sem,
            recv_sem=recv_sems.at[origin],
            device_id=device(target),
            device_id_type=pl.DeviceIdType.MESH,
        )
        copy.start()
        return copy

    def arrived(origin):
        pltpu.make_async_remote_copy(
            src_ref=buf.at[origin],
            dst_ref=buf.at[origin],
            send_sem=send_right.at[0],
            recv_sem=recv_sems.at[origin],
            device_id=device(right),
            device_id_type=pl.DeviceIdType.MESH,
        ).wait_recv()

    rightward = size // 2
    leftward = size - 1 - rightward
    sends = []
    for step in range(rightward):
        origin = lax.rem(me - step + size, size)
        if step > 0:
            arrived(origin)
        source = buf.at[origin]
        sends.append(send(source, origin, send_right.at[step], right))
        if step < leftward:
            origin = lax.rem(me + step, size)
            if step > 0:
                arrived(origin)
            source = buf.at[origin]
            sends.append(send(source, origin, send_left.at[step], left))
    arrived(lax.rem(me - rightward + size, size))
    if leftward > 0:
        arrived(lax.rem(me + leftward, size))
    for copy in sends:
        copy.wait_send()
    finish_row()
    o_ref[...] = buf[...]


def z_gather(value, size, x_size, collective_id):
    rightward = size // 2
    leftward = max(size - 1 - rightward, 1)
    row_shape = (x_size * value.shape[0],) + value.shape[1:]
    gathered = pl.pallas_call(
        lambda *refs: z_gather_kernel(size, x_size, *refs),
        out_shape=jax.ShapeDtypeStruct((size,) + row_shape, value.dtype),
        in_specs=[pl.BlockSpec(memory_space=pltpu.VMEM)],
        out_specs=pl.BlockSpec(memory_space=pltpu.VMEM),
        scratch_shapes=[
            pltpu.VMEM((size,) + row_shape, value.dtype),
            pltpu.SemaphoreType.DMA((rightward,)),
            pltpu.SemaphoreType.DMA((leftward,)),
            pltpu.SemaphoreType.DMA((size,)),
            pltpu.SemaphoreType.DMA((x_size,)),
            pltpu.SemaphoreType.DMA(()),
            pltpu.SemaphoreType.DMA((x_size,)),
        ],
        compiler_params=pltpu.CompilerParams(collective_id=collective_id, has_side_effects=True),
    )(value)
    return gathered.reshape((size * row_shape[0],) + value.shape[1:])


def z_project_kernel(size, x_size, steps, features, x_ref, mix_ref, blend_ref, w_ref,
                     decay_ref, terms_ref, buf, send_right, send_left, recv_sems,
                     x_sems, local_sem, send_x):
    me = lax.axis_index("z")
    right = lax.rem(me + 1, size)
    left = lax.rem(me + size - 1, size)
    hidden_start = (steps + 1) * features
    hidden_width = mix_ref.shape[1]
    decay_start = hidden_start + steps * hidden_width

    def device(position, column=None):
        column = lax.axis_index("x") if column is None else column
        return (position, column, lax.axis_index("narrow"))

    greet(device, me, left, right, x_size)
    finish_row = gather_row(x_ref, buf, x_sems, local_sem, send_x, device, me, x_size)

    def send(source, origin, sem, target):
        copy = pltpu.make_async_remote_copy(
            src_ref=source,
            dst_ref=buf.at[origin],
            send_sem=sem,
            recv_sem=recv_sems.at[origin],
            device_id=device(target),
            device_id_type=pl.DeviceIdType.MESH,
        )
        copy.start()
        return copy

    def arrived(origin):
        pltpu.make_async_remote_copy(
            src_ref=buf.at[origin],
            dst_ref=buf.at[origin],
            send_sem=send_right.at[0],
            recv_sem=recv_sems.at[origin],
            device_id=device(right),
            device_id_type=pl.DeviceIdType.MESH,
        ).wait_recv()

    def project(block, origin):
        selectors = w_ref.shape[0]
        for index in range(steps):
            previous = block[:, index * features : (index + 1) * features].astype(jnp.float32)
            normed = block[:, (index + 1) * features : (index + 2) * features].astype(jnp.float32)
            shifted = previous - normed
            hidden = block[:, hidden_start + index * hidden_width : hidden_start + (index + 1) * hidden_width]
            for selector in range(selectors):
                low_rank = jnp.dot(hidden, mix_ref[selector], preferred_element_type=jnp.float32)
                mixed = (
                    normed + shifted * (blend_ref[selector + 2 : selector + 3, :] + low_rank)
                ).astype(jnp.bfloat16)
                terms_ref[origin, index * selectors + selector] = jnp.dot(
                    mixed, w_ref[selector], preferred_element_type=jnp.float32
                ).astype(terms_ref.dtype)

    rightward = size // 2
    leftward = size - 1 - rightward
    sends = []
    for step in range(rightward):
        origin = lax.rem(me - step + size, size)
        if step > 0:
            arrived(origin)
        source = buf.at[origin]
        sends.append(send(source, origin, send_right.at[step], right))
        if step < leftward:
            other = lax.rem(me + step, size)
            if step > 0:
                arrived(other)
                sends.append(send(buf.at[other], other, send_left.at[step], left))
            else:
                sends.append(send(buf.at[other], other, send_left.at[step], left))
        project(source, origin)
        if 0 < step < leftward:
            project(buf.at[other], other)
    last_right = lax.rem(me - rightward + size, size)
    arrived(last_right)
    project(buf.at[last_right], last_right)
    if leftward > 0:
        last_left = lax.rem(me + leftward, size)
        arrived(last_left)
        project(buf.at[last_left], last_left)
    for copy in sends:
        copy.wait_send()
    finish_row()
    decay_ref[...] = buf[:, :, decay_start:]


def z_project(value, mix, blend, stacked, size, x_size, steps, features, collective_id):
    rightward = size // 2
    leftward = max(size - 1 - rightward, 1)
    rows, width = value.shape
    rows = rows * x_size
    selectors, _, out_width = stacked.shape
    decay_start = (steps + 1) * features + steps * mix.shape[1]
    return pl.pallas_call(
        lambda *refs: z_project_kernel(size, x_size, steps, features, *refs),
        out_shape=(
            jax.ShapeDtypeStruct((size, rows, width - decay_start), value.dtype),
            jax.ShapeDtypeStruct((size, steps * selectors, rows, out_width), jnp.bfloat16),
        ),
        in_specs=[pl.BlockSpec(memory_space=pltpu.VMEM)] * 4,
        out_specs=(pl.BlockSpec(memory_space=pltpu.VMEM), pl.BlockSpec(memory_space=pltpu.VMEM)),
        scratch_shapes=[
            pltpu.VMEM((size, rows, width), value.dtype),
            pltpu.SemaphoreType.DMA((rightward,)),
            pltpu.SemaphoreType.DMA((leftward,)),
            pltpu.SemaphoreType.DMA((size,)),
            pltpu.SemaphoreType.DMA((x_size,)),
            pltpu.SemaphoreType.DMA(()),
            pltpu.SemaphoreType.DMA((x_size,)),
        ],
        compiler_params=pltpu.CompilerParams(collective_id=collective_id, has_side_effects=True),
    )(value, mix, blend, stacked)


def per_device(
    sublevel_symbol_entries,
    prior_symbol_memory,
    entry_scaling_multiplier,
    entry_scaling_offset,
    learned_blending,
    blending_lowering_coefficients,
    blending_raising_coefficients,
    fading_lowering_coefficients,
    fading_raising_coefficients,
    learned_fading,
    immediate_item_premium,
    acceptor_projection,
    lookup_projection,
    payload_projection,
    gating_projection,
    emission_projection,
    group_scaling_multiplier,
    group_scaling_offset,
    dialogue_group_memory,
):
    rank = blending_raising_coefficients.shape[1]
    narrow_rows = dialogue_group_memory.shape[1]
    local_width = emission_projection.shape[1]
    group_partition = local_width // CHANNEL_SPAN
    sessions, steps, features = sublevel_symbol_entries.shape
    weights = (acceptor_projection, lookup_projection, payload_projection, gating_projection)

    floats = sublevel_symbol_entries.astype(jnp.float32)
    count = lax.axis_size("narrow")
    stats = narrow_sum(
        jnp.stack([jnp.sum(floats, -1), jnp.sum(floats * floats, -1)], 0), count, 0
    )
    center = stats[0][..., None] / FEATURE_EXTENT
    spread = stats[1][..., None] / FEATURE_EXTENT - center * center
    normed = (
        (floats - center) * lax.rsqrt(spread + 1e-05) * entry_scaling_multiplier
        + entry_scaling_offset
    ).astype(jnp.bfloat16)
    previous = jnp.concatenate([prior_symbol_memory[:, None], normed[:, :-1]], 1)
    normalized_float = normed.astype(jnp.float32)
    shifted_input = previous.astype(jnp.float32) - normalized_float
    blended = (normalized_float + shifted_input * learned_blending[0]).astype(jnp.bfloat16)
    partial_mix = jnp.einsum(
        "smd,dr->smr", blended, blending_lowering_coefficients,
        preferred_element_type=jnp.float32,
    )
    hidden_activation = jnp.tanh(narrow_sum(partial_mix, count, 1)).astype(jnp.bfloat16)
    decay_shift = jnp.einsum(
        "smr,rd->smd", hidden_activation[..., :rank], blending_raising_coefficients[0],
        preferred_element_type=jnp.float32,
    )
    decay_mix = (
        normalized_float + shifted_input * (learned_blending[1] + decay_shift)
    ).astype(jnp.bfloat16)
    partial_decay = jnp.einsum(
        "smd,dr->smr", decay_mix, fading_lowering_coefficients,
        preferred_element_type=jnp.float32,
    )
    decay_hidden = jnp.tanh(narrow_sum(partial_decay, count, 2)).astype(jnp.bfloat16)
    hidden_width = hidden_activation.shape[-1] - rank
    decay_width = decay_hidden.shape[-1]
    packed = jnp.concatenate(
        [prior_symbol_memory]
        + [normed[:, index] for index in range(steps)]
        + [
            hidden_activation[..., rank:].reshape(sessions, steps * hidden_width),
            decay_hidden.reshape(sessions, steps * decay_width),
        ],
        -1,
    )
    selectors = len(weights)
    mask = jnp.eye(selectors, dtype=blending_raising_coefficients.dtype)
    mix_stack = jnp.einsum(
        "ij,jrd->ijrd", mask, blending_raising_coefficients[1 : selectors + 1]
    ).reshape(selectors, selectors * rank, features)
    z_size = lax.axis_size("z")
    x_size = lax.axis_size("x")
    decay_all, terms = z_project(
        packed,
        mix_stack,
        learned_blending,
        jnp.stack(weights, 0),
        z_size,
        x_size,
        steps,
        features,
        3,
    )
    slots_per_device = z_size // lax.axis_size("narrow")
    projected = lax.psum_scatter(terms, "narrow", scatter_dimension=0, tiled=True)
    slot_rows = terms.shape[2]
    projected = (
        projected.reshape(slots_per_device, steps, selectors, slot_rows, local_width)
        .transpose(0, 3, 1, 2, 4)
        .reshape(narrow_rows, steps, selectors * local_width)
        .astype(jnp.float32)
    )

    rows_start = lax.axis_index("narrow") * narrow_rows
    own_rows = lax.dynamic_slice_in_dim(
        decay_all.reshape(-1, decay_all.shape[-1]), rows_start, narrow_rows, 0
    )
    decay_rows = own_rows.reshape(narrow_rows, steps, decay_width)
    decay_log = learned_fading + jnp.einsum(
        "smr,rd->smd", decay_rows, fading_raising_coefficients,
        preferred_element_type=jnp.float32,
    )
    shrink_coefficient = jnp.exp(-jnp.exp(decay_log))

    def channel_set_first(block):
        return block.reshape(narrow_rows, group_partition, CHANNEL_SPAN).transpose(1, 2, 0)

    state = dialogue_group_memory.reshape(group_partition, CHANNEL_SPAN, CHANNEL_SPAN, narrow_rows)
    reward = immediate_item_premium.reshape(group_partition, CHANNEL_SPAN)
    pieces = []
    for index in range(steps):
        acceptor = channel_set_first(projected[:, index, :local_width])
        key_now = channel_set_first(projected[:, index, local_width : 2 * local_width])
        value_now = channel_set_first(projected[:, index, 2 * local_width : 3 * local_width])
        gate_now = projected[:, index, 3 * local_width :]
        forget_now = channel_set_first(shrink_coefficient[:, index])
        dyadic = key_now[:, :, None, :] * value_now[:, None, :, :]
        retrieval = jnp.sum(
            acceptor[:, :, None, :] * (state + reward[:, :, None, None] * dyadic), 1
        )
        state = forget_now[:, :, None, :] * state + dyadic
        center_r = jnp.mean(retrieval, 1, keepdims=True)
        offset = retrieval - center_r
        scaled = offset * lax.rsqrt(jnp.mean(offset * offset, 1, keepdims=True) + 0.00064)
        squashed = scaled.transpose(2, 0, 1).reshape(narrow_rows, local_width)
        pieces.append(
            (
                (squashed * group_scaling_multiplier + group_scaling_offset)
                * jax.nn.silu(gate_now)
            ).astype(jnp.bfloat16)
        )
    gated = jnp.stack(pieces, 1).reshape(narrow_rows * steps, local_width).T
    gated_all = z_gather(gated, z_size, x_size, 4)
    mixing_output = (
        jnp.einsum(
            "cs,ce->se", gated_all, emission_projection, preferred_element_type=jnp.float32
        )
        .astype(jnp.bfloat16)
        .reshape(narrow_rows, steps, local_width)
    )
    return (
        mixing_output,
        state.reshape(group_partition * CHANNEL_SPAN * CHANNEL_SPAN, narrow_rows),
    )


def solution(mesh):
    wide_size = mesh.shape["wide"]
    x_size = 4 if wide_size % 4 == 0 else 1
    split = jax.sharding.Mesh(
        mesh.devices.reshape(wide_size // x_size, x_size, mesh.shape["narrow"]),
        ("z", "x", "narrow"),
    )
    wide = ("z", "x")
    placed = (
        P(wide, None, "narrow"),
        P(wide, "narrow"),
        P("narrow"),
        P("narrow"),
        P(None, "narrow"),
        P("narrow", None),
        P(None, None, "narrow"),
        P("narrow", None),
        P(None, wide),
        P(wide),
        P(wide),
        P("narrow", wide),
        P("narrow", wide),
        P("narrow", wide),
        P("narrow", wide),
        P(None, wide),
        P(wide),
        P(wide),
        P(wide, "narrow"),
    )
    return jax.shard_map(
        per_device,
        mesh=split,
        in_specs=placed,
        out_specs=(P("narrow", None, wide), P(wide, "narrow")),
        check_vma=False,
    )
```

```python
import jax
import jax.numpy as jnp
from jax import lax
from jax.sharding import PartitionSpec as P
from jax.experimental import pallas as pl
from jax.experimental.pallas import tpu as pltpu

CHANNEL_SPAN = 64
FEATURE_EXTENT = 4096


def narrow_sum_kernel(count, x_ref, o_ref, recv, send_sems, recv_sems):
    me = lax.axis_index("narrow")
    here = (lax.axis_index("z"), lax.axis_index("x"))

    def peer_id(peer):
        return here + (peer,)

    barrier = pltpu.get_barrier_semaphore()
    for peer in range(count):
        @pl.when(peer != me)
        def _():
            pl.semaphore_signal(
                barrier, 1, device_id=peer_id(peer), device_id_type=pl.DeviceIdType.MESH
            )
    pl.semaphore_wait(barrier, count - 1)

    def outgoing(peer):
        return pltpu.make_async_remote_copy(
            src_ref=x_ref,
            dst_ref=recv.at[me],
            send_sem=send_sems.at[peer],
            recv_sem=recv_sems.at[me],
            device_id=peer_id(peer),
            device_id_type=pl.DeviceIdType.MESH,
        )

    def incoming(peer):
        return pltpu.make_async_remote_copy(
            src_ref=x_ref,
            dst_ref=recv.at[peer],
            send_sem=send_sems.at[peer],
            recv_sem=recv_sems.at[peer],
            device_id=peer_id(peer),
            device_id_type=pl.DeviceIdType.MESH,
        )

    for peer in range(count):
        @pl.when(peer != me)
        def _():
            outgoing(peer).start()

    recv[me] = x_ref[...]
    for peer in range(count):
        @pl.when(peer != me)
        def _():
            outgoing(peer).wait_send()
            incoming(peer).wait_recv()

    total = recv[0]
    for peer in range(1, count):
        total = total + recv[peer]
    o_ref[...] = total


def narrow_sum(value, count, collective_id):
    shape = value.shape
    flat = value.reshape(-1, 128)
    summed = pl.pallas_call(
        lambda *refs: narrow_sum_kernel(count, *refs),
        out_shape=jax.ShapeDtypeStruct(flat.shape, flat.dtype),
        in_specs=[pl.BlockSpec(memory_space=pltpu.VMEM)],
        out_specs=pl.BlockSpec(memory_space=pltpu.VMEM),
        scratch_shapes=[
            pltpu.VMEM((count,) + flat.shape, flat.dtype),
            pltpu.SemaphoreType.DMA((count,)),
            pltpu.SemaphoreType.DMA((count,)),
        ],
        compiler_params=pltpu.CompilerParams(collective_id=collective_id, has_side_effects=True),
    )(flat)
    return summed.reshape(shape)


def gather_row(x_ref, buf, x_sems, local_sem, send_x, device, me, x_size):
    mine = lax.axis_index("x")
    rows = x_ref.shape[0]
    local = pltpu.make_async_copy(x_ref, buf.at[me, pl.ds(mine * rows, rows)], local_sem)
    local.start()
    sends = []
    for peer in range(x_size):
        @pl.when(peer != mine)
        def _():
            pltpu.make_async_remote_copy(
                src_ref=x_ref,
                dst_ref=buf.at[me, pl.ds(mine * rows, rows)],
                send_sem=send_x.at[peer],
                recv_sem=x_sems.at[mine],
                device_id=device(me, peer),
                device_id_type=pl.DeviceIdType.MESH,
            ).start()
    local.wait()
    for peer in range(x_size):
        @pl.when(peer != mine)
        def _():
            pltpu.make_async_remote_copy(
                src_ref=x_ref,
                dst_ref=buf.at[me, pl.ds(peer * rows, rows)],
                send_sem=send_x.at[peer],
                recv_sem=x_sems.at[peer],
                device_id=device(me, peer),
                device_id_type=pl.DeviceIdType.MESH,
            ).wait_recv()

    def finish():
        for peer in range(x_size):
            @pl.when(peer != mine)
            def _():
                pltpu.make_async_remote_copy(
                    src_ref=x_ref,
                    dst_ref=buf.at[me, pl.ds(mine * rows, rows)],
                    send_sem=send_x.at[peer],
                    recv_sem=x_sems.at[mine],
                    device_id=device(me, peer),
                    device_id_type=pl.DeviceIdType.MESH,
                ).wait_send()

    return finish


def greet(device, me, left, right, x_size, narrow_size=1):
    mine = lax.axis_index("x")
    here = lax.axis_index("narrow")
    barrier = pltpu.get_barrier_semaphore()
    for neighbour in (left, right):
        pl.semaphore_signal(
            barrier, 1, device_id=device(neighbour, mine), device_id_type=pl.DeviceIdType.MESH
        )
    for peer in range(x_size):
        @pl.when(peer != mine)
        def _():
            pl.semaphore_signal(
                barrier, 1, device_id=device(me, peer), device_id_type=pl.DeviceIdType.MESH
            )
    for peer in range(narrow_size if narrow_size > 1 else 0):
        @pl.when(peer != here)
        def _():
            pl.semaphore_signal(
                barrier, 1, device_id=(me, mine, peer), device_id_type=pl.DeviceIdType.MESH
            )
    pl.semaphore_wait(barrier, 2 + x_size - 1 + (narrow_size - 1 if narrow_size > 1 else 0))


def z_gather_kernel(size, x_size, x_ref, o_ref, buf, send_right, send_left, recv_sems,
                    x_sems, local_sem, send_x):
    me = lax.axis_index("z")
    right = lax.rem(me + 1, size)
    left = lax.rem(me + size - 1, size)

    def device(position, column=None):
        column = lax.axis_index("x") if column is None else column
        return (position, column, lax.axis_index("narrow"))

    greet(device, me, left, right, x_size)
    finish_row = gather_row(x_ref, buf, x_sems, local_sem, send_x, device, me, x_size)

    def send(source, origin, sem, target):
        copy = pltpu.make_async_remote_copy(
            src_ref=source,
            dst_ref=buf.at[origin],
            send_sem=sem,
            recv_sem=recv_sems.at[origin],
            device_id=device(target),
            device_id_type=pl.DeviceIdType.MESH,
        )
        copy.start()
        return copy

    def arrived(origin):
        pltpu.make_async_remote_copy(
            src_ref=buf.at[origin],
            dst_ref=buf.at[origin],
            send_sem=send_right.at[0],
            recv_sem=recv_sems.at[origin],
            device_id=device(right),
            device_id_type=pl.DeviceIdType.MESH,
        ).wait_recv()

    rightward = size // 2
    leftward = size - 1 - rightward
    sends = []
    for step in range(rightward):
        origin = lax.rem(me - step + size, size)
        if step > 0:
            arrived(origin)
        source = buf.at[origin]
        sends.append(send(source, origin, send_right.at[step], right))
        if step < leftward:
            origin = lax.rem(me + step, size)
            if step > 0:
                arrived(origin)
            source = buf.at[origin]
            sends.append(send(source, origin, send_left.at[step], left))
    arrived(lax.rem(me - rightward + size, size))
    if leftward > 0:
        arrived(lax.rem(me + leftward, size))
    for copy in sends:
        copy.wait_send()
    finish_row()
    o_ref[...] = buf[...]


def z_gather(value, size, x_size, collective_id):
    rightward = size // 2
    leftward = max(size - 1 - rightward, 1)
    row_shape = (x_size * value.shape[0],) + value.shape[1:]
    gathered = pl.pallas_call(
        lambda *refs: z_gather_kernel(size, x_size, *refs),
        out_shape=jax.ShapeDtypeStruct((size,) + row_shape, value.dtype),
        in_specs=[pl.BlockSpec(memory_space=pltpu.VMEM)],
        out_specs=pl.BlockSpec(memory_space=pltpu.VMEM),
        scratch_shapes=[
            pltpu.VMEM((size,) + row_shape, value.dtype),
            pltpu.SemaphoreType.DMA((rightward,)),
            pltpu.SemaphoreType.DMA((leftward,)),
            pltpu.SemaphoreType.DMA((size,)),
            pltpu.SemaphoreType.DMA((x_size,)),
            pltpu.SemaphoreType.DMA(()),
            pltpu.SemaphoreType.DMA((x_size,)),
        ],
        compiler_params=pltpu.CompilerParams(collective_id=collective_id, has_side_effects=True),
    )(value)
    return gathered.reshape((size * row_shape[0],) + value.shape[1:])


def z_project_kernel(size, x_size, steps, features, x_ref, mix_ref, blend_ref, w_ref,
                     decay_ref, sum_ref, buf, send_right, send_left, recv_sems,
                     x_sems, local_sem, send_x, terms_ref, parts, part_send, part_recv,
                     own_sems):
    me = lax.axis_index("z")
    right = lax.rem(me + 1, size)
    left = lax.rem(me + size - 1, size)
    hidden_start = (steps + 1) * features
    hidden_width = mix_ref.shape[1]
    decay_start = hidden_start + steps * hidden_width

    def device(position, column=None):
        column = lax.axis_index("x") if column is None else column
        return (position, column, lax.axis_index("narrow"))

    narrow_size, per_owner = parts.shape[0], parts.shape[1]
    mine = lax.axis_index("narrow")

    def owner_device(owner):
        return (me, lax.axis_index("x"), owner)

    greet(device, me, left, right, x_size, narrow_size)
    finish_row = gather_row(x_ref, buf, x_sems, local_sem, send_x, device, me, x_size)

    def part_copy(origin, owner):
        return pltpu.make_async_remote_copy(
            src_ref=terms_ref.at[origin],
            dst_ref=parts.at[mine, lax.rem(origin, per_owner)],
            send_sem=part_send.at[origin],
            recv_sem=part_recv.at[mine, lax.rem(origin, per_owner)],
            device_id=owner_device(owner),
            device_id_type=pl.DeviceIdType.MESH,
        )

    def ship(origin):
        owner = origin // per_owner

        @pl.when(owner != mine)
        def _():
            part_copy(origin, owner).start()

    def send(source, origin, sem, target):
        copy = pltpu.make_async_remote_copy(
            src_ref=source,
            dst_ref=buf.at[origin],
            send_sem=sem,
            recv_sem=recv_sems.at[origin],
            device_id=device(target),
            device_id_type=pl.DeviceIdType.MESH,
        )
        copy.start()
        return copy

    def arrived(origin):
        pltpu.make_async_remote_copy(
            src_ref=buf.at[origin],
            dst_ref=buf.at[origin],
            send_sem=send_right.at[0],
            recv_sem=recv_sems.at[origin],
            device_id=device(right),
            device_id_type=pl.DeviceIdType.MESH,
        ).wait_recv()

    def project(block, origin):
        selectors = w_ref.shape[0]
        for index in range(steps):
            previous = block[:, index * features : (index + 1) * features].astype(jnp.float32)
            normed = block[:, (index + 1) * features : (index + 2) * features].astype(jnp.float32)
            shifted = previous - normed
            hidden = block[:, hidden_start + index * hidden_width : hidden_start + (index + 1) * hidden_width]
            for selector in range(selectors):
                low_rank = jnp.dot(hidden, mix_ref[selector], preferred_element_type=jnp.float32)
                mixed = (
                    normed + shifted * (blend_ref[selector + 2 : selector + 3, :] + low_rank)
                ).astype(jnp.bfloat16)
                terms_ref[origin, index * selectors + selector] = jnp.dot(
                    mixed, w_ref[selector], preferred_element_type=jnp.float32
                ).astype(terms_ref.dtype)

    rightward = size // 2
    leftward = size - 1 - rightward
    sends = []
    for step in range(rightward):
        origin = lax.rem(me - step + size, size)
        if step > 0:
            arrived(origin)
        source = buf.at[origin]
        sends.append(send(source, origin, send_right.at[step], right))
        if step < leftward:
            other = lax.rem(me + step, size)
            if step > 0:
                arrived(other)
                sends.append(send(buf.at[other], other, send_left.at[step], left))
            else:
                sends.append(send(buf.at[other], other, send_left.at[step], left))
        project(source, origin)
        ship(origin)
        if 0 < step < leftward:
            project(buf.at[other], other)
            ship(other)
    last_right = lax.rem(me - rightward + size, size)
    arrived(last_right)
    project(buf.at[last_right], last_right)
    ship(last_right)
    if leftward > 0:
        last_left = lax.rem(me + leftward, size)
        arrived(last_left)
        project(buf.at[last_left], last_left)
        ship(last_left)
    own = []
    for slot in range(per_owner):
        copy = pltpu.make_async_copy(
            terms_ref.at[mine * per_owner + slot], parts.at[mine, slot], own_sems.at[slot]
        )
        copy.start()
        own.append(copy)
    for copy in sends:
        copy.wait_send()
    finish_row()
    decay_ref[...] = buf[:, :, decay_start:]
    for origin in range(size):
        @pl.when(origin // per_owner != mine)
        def _():
            part_copy(origin, origin // per_owner).wait_send()
    for source in range(narrow_size):
        @pl.when(source != mine)
        def _():
            for slot in range(per_owner):
                pltpu.make_async_remote_copy(
                    src_ref=parts.at[source, slot],
                    dst_ref=parts.at[source, slot],
                    send_sem=part_send.at[0],
                    recv_sem=part_recv.at[source, slot],
                    device_id=owner_device(source),
                    device_id_type=pl.DeviceIdType.MESH,
                ).wait_recv()
    for copy in own:
        copy.wait()
    for slot in range(per_owner):
        total = parts[0, slot].astype(jnp.float32)
        for source in range(1, narrow_size):
            total = total + parts[source, slot].astype(jnp.float32)
        sum_ref[slot] = total


def z_project(value, mix, blend, stacked, size, x_size, narrow_size, steps, features,
              collective_id):
    rightward = size // 2
    leftward = max(size - 1 - rightward, 1)
    rows, width = value.shape
    rows = rows * x_size
    selectors, _, out_width = stacked.shape
    decay_start = (steps + 1) * features + steps * mix.shape[1]
    per_owner = size // narrow_size
    term_shape = (steps * selectors, rows, out_width)
    return pl.pallas_call(
        lambda *refs: z_project_kernel(size, x_size, steps, features, *refs),
        out_shape=(
            jax.ShapeDtypeStruct((size, rows, width - decay_start), value.dtype),
            jax.ShapeDtypeStruct((per_owner,) + term_shape, jnp.float32),
        ),
        in_specs=[pl.BlockSpec(memory_space=pltpu.VMEM)] * 4,
        out_specs=(pl.BlockSpec(memory_space=pltpu.VMEM), pl.BlockSpec(memory_space=pltpu.VMEM)),
        scratch_shapes=[
            pltpu.VMEM((size, rows, width), value.dtype),
            pltpu.SemaphoreType.DMA((rightward,)),
            pltpu.SemaphoreType.DMA((leftward,)),
            pltpu.SemaphoreType.DMA((size,)),
            pltpu.SemaphoreType.DMA((x_size,)),
            pltpu.SemaphoreType.DMA(()),
            pltpu.SemaphoreType.DMA((x_size,)),
            pltpu.VMEM((size,) + term_shape, jnp.bfloat16),
            pltpu.VMEM((narrow_size, per_owner) + term_shape, jnp.bfloat16),
            pltpu.SemaphoreType.DMA((size,)),
            pltpu.SemaphoreType.DMA((narrow_size, per_owner)),
            pltpu.SemaphoreType.DMA((per_owner,)),
        ],
        compiler_params=pltpu.CompilerParams(collective_id=collective_id, has_side_effects=True),
    )(value, mix, blend, stacked)


def per_device(
    sublevel_symbol_entries,
    prior_symbol_memory,
    entry_scaling_multiplier,
    entry_scaling_offset,
    learned_blending,
    blending_lowering_coefficients,
    blending_raising_coefficients,
    fading_lowering_coefficients,
    fading_raising_coefficients,
    learned_fading,
    immediate_item_premium,
    acceptor_projection,
    lookup_projection,
    payload_projection,
    gating_projection,
    emission_projection,
    group_scaling_multiplier,
    group_scaling_offset,
    dialogue_group_memory,
):
    rank = blending_raising_coefficients.shape[1]
    narrow_rows = dialogue_group_memory.shape[1]
    local_width = emission_projection.shape[1]
    group_partition = local_width // CHANNEL_SPAN
    sessions, steps, features = sublevel_symbol_entries.shape
    weights = (acceptor_projection, lookup_projection, payload_projection, gating_projection)

    floats = sublevel_symbol_entries.astype(jnp.float32)
    count = lax.axis_size("narrow")
    stats = narrow_sum(
        jnp.stack([jnp.sum(floats, -1), jnp.sum(floats * floats, -1)], 0), count, 0
    )
    center = stats[0][..., None] / FEATURE_EXTENT
    spread = stats[1][..., None] / FEATURE_EXTENT - center * center
    normed = (
        (floats - center) * lax.rsqrt(spread + 1e-05) * entry_scaling_multiplier
        + entry_scaling_offset
    ).astype(jnp.bfloat16)
    previous = jnp.concatenate([prior_symbol_memory[:, None], normed[:, :-1]], 1)
    normalized_float = normed.astype(jnp.float32)
    shifted_input = previous.astype(jnp.float32) - normalized_float
    blended = (normalized_float + shifted_input * learned_blending[0]).astype(jnp.bfloat16)
    partial_mix = jnp.einsum(
        "smd,dr->smr", blended, blending_lowering_coefficients,
        preferred_element_type=jnp.float32,
    )
    hidden_activation = jnp.tanh(narrow_sum(partial_mix, count, 1)).astype(jnp.bfloat16)
    decay_shift = jnp.einsum(
        "smr,rd->smd", hidden_activation[..., :rank], blending_raising_coefficients[0],
        preferred_element_type=jnp.float32,
    )
    decay_mix = (
        normalized_float + shifted_input * (learned_blending[1] + decay_shift)
    ).astype(jnp.bfloat16)
    partial_decay = jnp.einsum(
        "smd,dr->smr", decay_mix, fading_lowering_coefficients,
        preferred_element_type=jnp.float32,
    )
    decay_hidden = jnp.tanh(narrow_sum(partial_decay, count, 2)).astype(jnp.bfloat16)
    hidden_width = hidden_activation.shape[-1] - rank
    decay_width = decay_hidden.shape[-1]
    packed = jnp.concatenate(
        [prior_symbol_memory]
        + [normed[:, index] for index in range(steps)]
        + [
            hidden_activation[..., rank:].reshape(sessions, steps * hidden_width),
            decay_hidden.reshape(sessions, steps * decay_width),
        ],
        -1,
    )
    selectors = len(weights)
    mask = jnp.eye(selectors, dtype=blending_raising_coefficients.dtype)
    mix_stack = jnp.einsum(
        "ij,jrd->ijrd", mask, blending_raising_coefficients[1 : selectors + 1]
    ).reshape(selectors, selectors * rank, features)
    z_size = lax.axis_size("z")
    x_size = lax.axis_size("x")
    narrow_size = lax.axis_size("narrow")
    decay_all, summed = z_project(
        packed,
        mix_stack,
        learned_blending,
        jnp.stack(weights, 0),
        z_size,
        x_size,
        narrow_size,
        steps,
        features,
        3,
    )
    per_owner = z_size // narrow_size
    slot_rows = summed.shape[2]
    projected = (
        summed.reshape(per_owner, steps, selectors, slot_rows, local_width)
        .transpose(0, 3, 1, 2, 4)
        .reshape(narrow_rows, steps, selectors * local_width)
    )

    rows_start = lax.axis_index("narrow") * narrow_rows
    own_rows = lax.dynamic_slice_in_dim(
        decay_all.reshape(-1, decay_all.shape[-1]), rows_start, narrow_rows, 0
    )
    decay_rows = own_rows.reshape(narrow_rows, steps, decay_width)
    decay_log = learned_fading + jnp.einsum(
        "smr,rd->smd", decay_rows, fading_raising_coefficients,
        preferred_element_type=jnp.float32,
    )
    shrink_coefficient = jnp.exp(-jnp.exp(decay_log))

    def channel_set_first(block):
        return block.reshape(narrow_rows, group_partition, CHANNEL_SPAN).transpose(1, 2, 0)

    state = dialogue_group_memory.reshape(group_partition, CHANNEL_SPAN, CHANNEL_SPAN, narrow_rows)
    reward = immediate_item_premium.reshape(group_partition, CHANNEL_SPAN)
    pieces = []
    for index in range(steps):
        acceptor = channel_set_first(projected[:, index, :local_width])
        key_now = channel_set_first(projected[:, index, local_width : 2 * local_width])
        value_now = channel_set_first(projected[:, index, 2 * local_width : 3 * local_width])
        gate_now = projected[:, index, 3 * local_width :]
        forget_now = channel_set_first(shrink_coefficient[:, index])
        dyadic = key_now[:, :, None, :] * value_now[:, None, :, :]
        retrieval = jnp.sum(
            acceptor[:, :, None, :] * (state + reward[:, :, None, None] * dyadic), 1
        )
        state = forget_now[:, :, None, :] * state + dyadic
        center_r = jnp.mean(retrieval, 1, keepdims=True)
        offset = retrieval - center_r
        scaled = offset * lax.rsqrt(jnp.mean(offset * offset, 1, keepdims=True) + 0.00064)
        squashed = scaled.transpose(2, 0, 1).reshape(narrow_rows, local_width)
        pieces.append(
            (
                (squashed * group_scaling_multiplier + group_scaling_offset)
                * jax.nn.silu(gate_now)
            ).astype(jnp.bfloat16)
        )
    gated = jnp.stack(pieces, 1).reshape(narrow_rows * steps, local_width).T
    gated_all = z_gather(gated, z_size, x_size, 4)
    mixing_output = (
        jnp.einsum(
            "cs,ce->se", gated_all, emission_projection, preferred_element_type=jnp.float32
        )
        .astype(jnp.bfloat16)
        .reshape(narrow_rows, steps, local_width)
    )
    return (
        mixing_output,
        state.reshape(group_partition * CHANNEL_SPAN * CHANNEL_SPAN, narrow_rows),
    )


def solution(mesh):
    wide_size = mesh.shape["wide"]
    x_size = 4 if wide_size % 4 == 0 else 1
    split = jax.sharding.Mesh(
        mesh.devices.reshape(wide_size // x_size, x_size, mesh.shape["narrow"]),
        ("z", "x", "narrow"),
    )
    wide = ("z", "x")
    placed = (
        P(wide, None, "narrow"),
        P(wide, "narrow"),
        P("narrow"),
        P("narrow"),
        P(None, "narrow"),
        P("narrow", None),
        P(None, None, "narrow"),
        P("narrow", None),
        P(None, wide),
        P(wide),
        P(wide),
        P("narrow", wide),
        P("narrow", wide),
        P("narrow", wide),
        P("narrow", wide),
        P(None, wide),
        P(wide),
        P(wide),
        P(wide, "narrow"),
    )
    return jax.shard_map(
        per_device,
        mesh=split,
        in_specs=placed,
        out_specs=(P("narrow", None, wide), P(wide, "narrow")),
        check_vma=False,
    )
```

```python
import jax
import jax.numpy as jnp
from jax import lax
from jax.sharding import PartitionSpec as P
from jax.experimental import pallas as pl
from jax.experimental.pallas import tpu as pltpu

CHANNEL_SPAN = 64
FEATURE_EXTENT = 4096
PIECES = 2


def narrow_sum_kernel(count, x_ref, o_ref, recv, send_sems, recv_sems):
    me = lax.axis_index("narrow")
    here = (lax.axis_index("z"), lax.axis_index("x"))

    def peer_id(peer):
        return here + (peer,)

    barrier = pltpu.get_barrier_semaphore()
    for peer in range(count):
        @pl.when(peer != me)
        def _():
            pl.semaphore_signal(
                barrier, 1, device_id=peer_id(peer), device_id_type=pl.DeviceIdType.MESH
            )
    pl.semaphore_wait(barrier, count - 1)

    def outgoing(peer):
        return pltpu.make_async_remote_copy(
            src_ref=x_ref,
            dst_ref=recv.at[me],
            send_sem=send_sems.at[peer],
            recv_sem=recv_sems.at[me],
            device_id=peer_id(peer),
            device_id_type=pl.DeviceIdType.MESH,
        )

    def incoming(peer):
        return pltpu.make_async_remote_copy(
            src_ref=x_ref,
            dst_ref=recv.at[peer],
            send_sem=send_sems.at[peer],
            recv_sem=recv_sems.at[peer],
            device_id=peer_id(peer),
            device_id_type=pl.DeviceIdType.MESH,
        )

    for peer in range(count):
        @pl.when(peer != me)
        def _():
            outgoing(peer).start()

    recv[me] = x_ref[...]
    for peer in range(count):
        @pl.when(peer != me)
        def _():
            outgoing(peer).wait_send()
            incoming(peer).wait_recv()

    total = recv[0]
    for peer in range(1, count):
        total = total + recv[peer]
    o_ref[...] = total


def narrow_sum(value, count, collective_id):
    shape = value.shape
    flat = value.reshape(-1, 128)
    summed = pl.pallas_call(
        lambda *refs: narrow_sum_kernel(count, *refs),
        out_shape=jax.ShapeDtypeStruct(flat.shape, flat.dtype),
        in_specs=[pl.BlockSpec(memory_space=pltpu.VMEM)],
        out_specs=pl.BlockSpec(memory_space=pltpu.VMEM),
        scratch_shapes=[
            pltpu.VMEM((count,) + flat.shape, flat.dtype),
            pltpu.SemaphoreType.DMA((count,)),
            pltpu.SemaphoreType.DMA((count,)),
        ],
        compiler_params=pltpu.CompilerParams(collective_id=collective_id, has_side_effects=True),
    )(flat)
    return summed.reshape(shape)


def gather_row(x_ref, buf, x_sems, local_sem, send_x, device, me, x_size):
    mine = lax.axis_index("x")
    rows = x_ref.shape[0]
    local = pltpu.make_async_copy(x_ref, buf.at[me, pl.ds(mine * rows, rows)], local_sem)
    local.start()
    sends = []
    for peer in range(x_size):
        @pl.when(peer != mine)
        def _():
            pltpu.make_async_remote_copy(
                src_ref=x_ref,
                dst_ref=buf.at[me, pl.ds(mine * rows, rows)],
                send_sem=send_x.at[peer],
                recv_sem=x_sems.at[mine],
                device_id=device(me, peer),
                device_id_type=pl.DeviceIdType.MESH,
            ).start()
    local.wait()
    for peer in range(x_size):
        @pl.when(peer != mine)
        def _():
            pltpu.make_async_remote_copy(
                src_ref=x_ref,
                dst_ref=buf.at[me, pl.ds(peer * rows, rows)],
                send_sem=send_x.at[peer],
                recv_sem=x_sems.at[peer],
                device_id=device(me, peer),
                device_id_type=pl.DeviceIdType.MESH,
            ).wait_recv()

    def finish():
        for peer in range(x_size):
            @pl.when(peer != mine)
            def _():
                pltpu.make_async_remote_copy(
                    src_ref=x_ref,
                    dst_ref=buf.at[me, pl.ds(mine * rows, rows)],
                    send_sem=send_x.at[peer],
                    recv_sem=x_sems.at[mine],
                    device_id=device(me, peer),
                    device_id_type=pl.DeviceIdType.MESH,
                ).wait_send()

    return finish


def greet(device, me, left, right, x_size, narrow_size=1):
    mine = lax.axis_index("x")
    here = lax.axis_index("narrow")
    barrier = pltpu.get_barrier_semaphore()
    for neighbour in (left, right):
        pl.semaphore_signal(
            barrier, 1, device_id=device(neighbour, mine), device_id_type=pl.DeviceIdType.MESH
        )
    for peer in range(x_size):
        @pl.when(peer != mine)
        def _():
            pl.semaphore_signal(
                barrier, 1, device_id=device(me, peer), device_id_type=pl.DeviceIdType.MESH
            )
    for peer in range(narrow_size if narrow_size > 1 else 0):
        @pl.when(peer != here)
        def _():
            pl.semaphore_signal(
                barrier, 1, device_id=(me, mine, peer), device_id_type=pl.DeviceIdType.MESH
            )
    pl.semaphore_wait(barrier, 2 + x_size - 1 + (narrow_size - 1 if narrow_size > 1 else 0))


def run_ring(buf, me, size, left, right, device, send_right, send_left, recv_sems, on_slot):
    pieces = recv_sems.shape[1]
    part = buf.shape[1] // pieces

    def view(origin, piece):
        return buf.at[origin, pl.ds(piece * part, part)]

    def send(origin, piece, sem, target):
        copy = pltpu.make_async_remote_copy(
            src_ref=view(origin, piece),
            dst_ref=view(origin, piece),
            send_sem=sem,
            recv_sem=recv_sems.at[origin, piece],
            device_id=device(target),
            device_id_type=pl.DeviceIdType.MESH,
        )
        copy.start()
        return copy

    def arrived(origin, piece):
        pltpu.make_async_remote_copy(
            src_ref=view(origin, piece),
            dst_ref=view(origin, piece),
            send_sem=send_right.at[0, 0],
            recv_sem=recv_sems.at[origin, piece],
            device_id=device(right),
            device_id_type=pl.DeviceIdType.MESH,
        ).wait_recv()

    rightward = size // 2
    leftward = size - 1 - rightward
    sends = []
    for step in range(rightward):
        right_origin = lax.rem(me - step + size, size)
        left_origin = lax.rem(me + step, size) if step < leftward else None
        for piece in range(pieces):
            if step > 0:
                arrived(right_origin, piece)
            sends.append(send(right_origin, piece, send_right.at[step, piece], right))
            if left_origin is not None:
                if step > 0:
                    arrived(left_origin, piece)
                sends.append(send(left_origin, piece, send_left.at[step, piece], left))
        on_slot(right_origin)
        if left_origin is not None and step > 0:
            on_slot(left_origin)
    last_right = lax.rem(me - rightward + size, size)
    for piece in range(pieces):
        arrived(last_right, piece)
    on_slot(last_right)
    if leftward > 0:
        last_left = lax.rem(me + leftward, size)
        for piece in range(pieces):
            arrived(last_left, piece)
        on_slot(last_left)
    return sends


def z_gather_kernel(size, x_size, x_ref, o_ref, buf, send_right, send_left, recv_sems,
                    x_sems, local_sem, send_x):
    me = lax.axis_index("z")
    right = lax.rem(me + 1, size)
    left = lax.rem(me + size - 1, size)

    def device(position, column=None):
        column = lax.axis_index("x") if column is None else column
        return (position, column, lax.axis_index("narrow"))

    greet(device, me, left, right, x_size)
    finish_row = gather_row(x_ref, buf, x_sems, local_sem, send_x, device, me, x_size)

    sends = run_ring(
        buf, me, size, left, right, device, send_right, send_left, recv_sems, lambda origin: None
    )
    for copy in sends:
        copy.wait_send()
    finish_row()
    o_ref[...] = buf[...]


def z_gather(value, size, x_size, collective_id):
    rightward = size // 2
    leftward = max(size - 1 - rightward, 1)
    row_shape = (x_size * value.shape[0],) + value.shape[1:]
    gathered = pl.pallas_call(
        lambda *refs: z_gather_kernel(size, x_size, *refs),
        out_shape=jax.ShapeDtypeStruct((size,) + row_shape, value.dtype),
        in_specs=[pl.BlockSpec(memory_space=pltpu.VMEM)],
        out_specs=pl.BlockSpec(memory_space=pltpu.VMEM),
        scratch_shapes=[
            pltpu.VMEM((size,) + row_shape, value.dtype),
            pltpu.SemaphoreType.DMA((rightward, PIECES)),
            pltpu.SemaphoreType.DMA((leftward, PIECES)),
            pltpu.SemaphoreType.DMA((size, PIECES)),
            pltpu.SemaphoreType.DMA((x_size,)),
            pltpu.SemaphoreType.DMA(()),
            pltpu.SemaphoreType.DMA((x_size,)),
        ],
        compiler_params=pltpu.CompilerParams(collective_id=collective_id, has_side_effects=True),
    )(value)
    return gathered.reshape((size * row_shape[0],) + value.shape[1:])


def z_project_kernel(size, x_size, steps, features, x_ref, mix_ref, blend_ref, w_ref,
                     decay_ref, sum_ref, buf, send_right, send_left, recv_sems,
                     x_sems, local_sem, send_x, terms_ref, parts, part_send, part_recv,
                     own_sems):
    me = lax.axis_index("z")
    right = lax.rem(me + 1, size)
    left = lax.rem(me + size - 1, size)
    hidden_start = (steps + 1) * features
    hidden_width = mix_ref.shape[1]
    decay_start = hidden_start + steps * hidden_width

    def device(position, column=None):
        column = lax.axis_index("x") if column is None else column
        return (position, column, lax.axis_index("narrow"))

    narrow_size, per_owner = parts.shape[0], parts.shape[1]
    mine = lax.axis_index("narrow")

    def owner_device(owner):
        return (me, lax.axis_index("x"), owner)

    greet(device, me, left, right, x_size, narrow_size)
    finish_row = gather_row(x_ref, buf, x_sems, local_sem, send_x, device, me, x_size)

    def part_copy(origin, owner):
        return pltpu.make_async_remote_copy(
            src_ref=terms_ref.at[origin],
            dst_ref=parts.at[mine, lax.rem(origin, per_owner)],
            send_sem=part_send.at[origin],
            recv_sem=part_recv.at[mine, lax.rem(origin, per_owner)],
            device_id=owner_device(owner),
            device_id_type=pl.DeviceIdType.MESH,
        )

    def ship(origin):
        owner = origin // per_owner

        @pl.when(owner != mine)
        def _():
            part_copy(origin, owner).start()

    def project(block, origin):
        selectors = w_ref.shape[0]
        for index in range(steps):
            previous = block[:, index * features : (index + 1) * features].astype(jnp.float32)
            normed = block[:, (index + 1) * features : (index + 2) * features].astype(jnp.float32)
            shifted = previous - normed
            hidden = block[:, hidden_start + index * hidden_width : hidden_start + (index + 1) * hidden_width]
            for selector in range(selectors):
                low_rank = jnp.dot(hidden, mix_ref[selector], preferred_element_type=jnp.float32)
                mixed = (
                    normed + shifted * (blend_ref[selector + 2 : selector + 3, :] + low_rank)
                ).astype(jnp.bfloat16)
                terms_ref[origin, index * selectors + selector] = jnp.dot(
                    mixed, w_ref[selector], preferred_element_type=jnp.float32
                ).astype(terms_ref.dtype)

    def on_slot(origin):
        project(buf.at[origin], origin)
        ship(origin)

    sends = run_ring(
        buf, me, size, left, right, device, send_right, send_left, recv_sems, on_slot
    )
    own = []
    for slot in range(per_owner):
        copy = pltpu.make_async_copy(
            terms_ref.at[mine * per_owner + slot], parts.at[mine, slot], own_sems.at[slot]
        )
        copy.start()
        own.append(copy)
    for copy in sends:
        copy.wait_send()
    finish_row()
    decay_ref[...] = buf[:, :, decay_start:]
    for origin in range(size):
        @pl.when(origin // per_owner != mine)
        def _():
            part_copy(origin, origin // per_owner).wait_send()
    for source in range(narrow_size):
        @pl.when(source != mine)
        def _():
            for slot in range(per_owner):
                pltpu.make_async_remote_copy(
                    src_ref=parts.at[source, slot],
                    dst_ref=parts.at[source, slot],
                    send_sem=part_send.at[0],
                    recv_sem=part_recv.at[source, slot],
                    device_id=owner_device(source),
                    device_id_type=pl.DeviceIdType.MESH,
                ).wait_recv()
    for copy in own:
        copy.wait()
    for slot in range(per_owner):
        total = parts[0, slot].astype(jnp.float32)
        for source in range(1, narrow_size):
            total = total + parts[source, slot].astype(jnp.float32)
        sum_ref[slot] = total


def z_project(value, mix, blend, stacked, size, x_size, narrow_size, steps, features,
              collective_id):
    rightward = size // 2
    leftward = max(size - 1 - rightward, 1)
    rows, width = value.shape
    rows = rows * x_size
    selectors, _, out_width = stacked.shape
    decay_start = (steps + 1) * features + steps * mix.shape[1]
    per_owner = size // narrow_size
    term_shape = (steps * selectors, rows, out_width)
    return pl.pallas_call(
        lambda *refs: z_project_kernel(size, x_size, steps, features, *refs),
        out_shape=(
            jax.ShapeDtypeStruct((size, rows, width - decay_start), value.dtype),
            jax.ShapeDtypeStruct((per_owner,) + term_shape, jnp.float32),
        ),
        in_specs=[pl.BlockSpec(memory_space=pltpu.VMEM)] * 4,
        out_specs=(pl.BlockSpec(memory_space=pltpu.VMEM), pl.BlockSpec(memory_space=pltpu.VMEM)),
        scratch_shapes=[
            pltpu.VMEM((size, rows, width), value.dtype),
            pltpu.SemaphoreType.DMA((rightward, PIECES)),
            pltpu.SemaphoreType.DMA((leftward, PIECES)),
            pltpu.SemaphoreType.DMA((size, PIECES)),
            pltpu.SemaphoreType.DMA((x_size,)),
            pltpu.SemaphoreType.DMA(()),
            pltpu.SemaphoreType.DMA((x_size,)),
            pltpu.VMEM((size,) + term_shape, jnp.bfloat16),
            pltpu.VMEM((narrow_size, per_owner) + term_shape, jnp.bfloat16),
            pltpu.SemaphoreType.DMA((size,)),
            pltpu.SemaphoreType.DMA((narrow_size, per_owner)),
            pltpu.SemaphoreType.DMA((per_owner,)),
        ],
        compiler_params=pltpu.CompilerParams(collective_id=collective_id, has_side_effects=True),
    )(value, mix, blend, stacked)


def per_device(
    sublevel_symbol_entries,
    prior_symbol_memory,
    entry_scaling_multiplier,
    entry_scaling_offset,
    learned_blending,
    blending_lowering_coefficients,
    blending_raising_coefficients,
    fading_lowering_coefficients,
    fading_raising_coefficients,
    learned_fading,
    immediate_item_premium,
    acceptor_projection,
    lookup_projection,
    payload_projection,
    gating_projection,
    emission_projection,
    group_scaling_multiplier,
    group_scaling_offset,
    dialogue_group_memory,
):
    rank = blending_raising_coefficients.shape[1]
    narrow_rows = dialogue_group_memory.shape[1]
    local_width = emission_projection.shape[1]
    group_partition = local_width // CHANNEL_SPAN
    sessions, steps, features = sublevel_symbol_entries.shape
    weights = (acceptor_projection, lookup_projection, payload_projection, gating_projection)

    floats = sublevel_symbol_entries.astype(jnp.float32)
    count = lax.axis_size("narrow")
    stats = narrow_sum(
        jnp.stack([jnp.sum(floats, -1), jnp.sum(floats * floats, -1)], 0), count, 0
    )
    center = stats[0][..., None] / FEATURE_EXTENT
    spread = stats[1][..., None] / FEATURE_EXTENT - center * center
    normed = (
        (floats - center) * lax.rsqrt(spread + 1e-05) * entry_scaling_multiplier
        + entry_scaling_offset
    ).astype(jnp.bfloat16)
    previous = jnp.concatenate([prior_symbol_memory[:, None], normed[:, :-1]], 1)
    normalized_float = normed.astype(jnp.float32)
    shifted_input = previous.astype(jnp.float32) - normalized_float
    blended = (normalized_float + shifted_input * learned_blending[0]).astype(jnp.bfloat16)
    partial_mix = jnp.einsum(
        "smd,dr->smr", blended, blending_lowering_coefficients,
        preferred_element_type=jnp.float32,
    )
    hidden_activation = jnp.tanh(narrow_sum(partial_mix, count, 1)).astype(jnp.bfloat16)
    decay_shift = jnp.einsum(
        "smr,rd->smd", hidden_activation[..., :rank], blending_raising_coefficients[0],
        preferred_element_type=jnp.float32,
    )
    decay_mix = (
        normalized_float + shifted_input * (learned_blending[1] + decay_shift)
    ).astype(jnp.bfloat16)
    partial_decay = jnp.einsum(
        "smd,dr->smr", decay_mix, fading_lowering_coefficients,
        preferred_element_type=jnp.float32,
    )
    decay_hidden = jnp.tanh(narrow_sum(partial_decay, count, 2)).astype(jnp.bfloat16)
    hidden_width = hidden_activation.shape[-1] - rank
    decay_width = decay_hidden.shape[-1]
    packed = jnp.concatenate(
        [prior_symbol_memory]
        + [normed[:, index] for index in range(steps)]
        + [
            hidden_activation[..., rank:].reshape(sessions, steps * hidden_width),
            decay_hidden.reshape(sessions, steps * decay_width),
        ],
        -1,
    )
    selectors = len(weights)
    mask = jnp.eye(selectors, dtype=blending_raising_coefficients.dtype)
    mix_stack = jnp.einsum(
        "ij,jrd->ijrd", mask, blending_raising_coefficients[1 : selectors + 1]
    ).reshape(selectors, selectors * rank, features)
    z_size = lax.axis_size("z")
    x_size = lax.axis_size("x")
    narrow_size = lax.axis_size("narrow")
    decay_all, summed = z_project(
        packed,
        mix_stack,
        learned_blending,
        jnp.stack(weights, 0),
        z_size,
        x_size,
        narrow_size,
        steps,
        features,
        3,
    )
    per_owner = z_size // narrow_size
    slot_rows = summed.shape[2]
    projected = (
        summed.reshape(per_owner, steps, selectors, slot_rows, local_width)
        .transpose(0, 3, 1, 2, 4)
        .reshape(narrow_rows, steps, selectors * local_width)
    )

    rows_start = lax.axis_index("narrow") * narrow_rows
    own_rows = lax.dynamic_slice_in_dim(
        decay_all.reshape(-1, decay_all.shape[-1]), rows_start, narrow_rows, 0
    )
    decay_rows = own_rows.reshape(narrow_rows, steps, decay_width)
    decay_log = learned_fading + jnp.einsum(
        "smr,rd->smd", decay_rows, fading_raising_coefficients,
        preferred_element_type=jnp.float32,
    )
    shrink_coefficient = jnp.exp(-jnp.exp(decay_log))

    def channel_set_first(block):
        return block.reshape(narrow_rows, group_partition, CHANNEL_SPAN).transpose(1, 2, 0)

    state = dialogue_group_memory.reshape(group_partition, CHANNEL_SPAN, CHANNEL_SPAN, narrow_rows)
    reward = immediate_item_premium.reshape(group_partition, CHANNEL_SPAN)
    pieces = []
    for index in range(steps):
        acceptor = channel_set_first(projected[:, index, :local_width])
        key_now = channel_set_first(projected[:, index, local_width : 2 * local_width])
        value_now = channel_set_first(projected[:, index, 2 * local_width : 3 * local_width])
        gate_now = projected[:, index, 3 * local_width :]
        forget_now = channel_set_first(shrink_coefficient[:, index])
        dyadic = key_now[:, :, None, :] * value_now[:, None, :, :]
        retrieval = jnp.sum(
            acceptor[:, :, None, :] * (state + reward[:, :, None, None] * dyadic), 1
        )
        state = forget_now[:, :, None, :] * state + dyadic
        center_r = jnp.mean(retrieval, 1, keepdims=True)
        offset = retrieval - center_r
        scaled = offset * lax.rsqrt(jnp.mean(offset * offset, 1, keepdims=True) + 0.00064)
        squashed = scaled.transpose(2, 0, 1).reshape(narrow_rows, local_width)
        pieces.append(
            (
                (squashed * group_scaling_multiplier + group_scaling_offset)
                * jax.nn.silu(gate_now)
            ).astype(jnp.bfloat16)
        )
    gated = jnp.stack(pieces, 1).reshape(narrow_rows * steps, local_width).T
    gated_all = z_gather(gated, z_size, x_size, 4)
    mixing_output = (
        jnp.einsum(
            "cs,ce->se", gated_all, emission_projection, preferred_element_type=jnp.float32
        )
        .astype(jnp.bfloat16)
        .reshape(narrow_rows, steps, local_width)
    )
    return (
        mixing_output,
        state.reshape(group_partition * CHANNEL_SPAN * CHANNEL_SPAN, narrow_rows),
    )


def solution(mesh):
    wide_size = mesh.shape["wide"]
    x_size = 4 if wide_size % 4 == 0 else 1
    split = jax.sharding.Mesh(
        mesh.devices.reshape(wide_size // x_size, x_size, mesh.shape["narrow"]),
        ("z", "x", "narrow"),
    )
    wide = ("z", "x")
    placed = (
        P(wide, None, "narrow"),
        P(wide, "narrow"),
        P("narrow"),
        P("narrow"),
        P(None, "narrow"),
        P("narrow", None),
        P(None, None, "narrow"),
        P("narrow", None),
        P(None, wide),
        P(wide),
        P(wide),
        P("narrow", wide),
        P("narrow", wide),
        P("narrow", wide),
        P("narrow", wide),
        P(None, wide),
        P(wide),
        P(wide),
        P(wide, "narrow"),
    )
    return jax.shard_map(
        per_device,
        mesh=split,
        in_specs=placed,
        out_specs=(P("narrow", None, wide), P(wide, "narrow")),
        check_vma=False,
    )
```
